512 devices in a mesh: port: 16 (over y_lo, x), tile: 32 (over y_hi, z, core).
Axes of the slice: x: 4, y: 8 (y_hi: 2, y_lo: 4; y = y_hi * 4 + y_lo), z: 8, core: 2. Of those that a mesh axis runs over, the one named last changes fastest.
Arguments:
- electric: float32 [16, 3, 6, 512, 640], P('port', None, None, 'tile'), may hold values from -6 to 6
- magnetic: float32 [16, 3, 6, 512, 640], P('port', None, None, 'tile'), may hold values from -6 to 6
- adjoint_electric: float32 [16, 3, 6, 512, 640], P('port', None, None, 'tile'), may hold values from -6 to 6
- adjoint_magnetic: float32 [16, 3, 6, 512, 640], P('port', None, None, 'tile'), may hold values from -6 to 6
- region_labels: int32 [6, 512, 640], P(None, 'tile'), may hold values from 0 to 7
- permittivity_table: float32 [8], replicated, may hold values from 1 to 12
- conductivity_table: float32 [8], replicated, may hold values from 0.05 to 2
- port_cells: int32 [16], P('port'), may hold values from 0 to 1966079
- port_amplitude: float32 [16, 3], P('port'), may hold values from -8 to 8
Outputs:
- earlier_electric: float32 [16, 3, 6, 512, 640], P('port', None, None, 'tile')
- earlier_magnetic: float32 [16, 3, 6, 512, 640], P('port', None, None, 'tile')
- gradient_permittivity: float32 [6, 512, 640], P(None, 'tile', 'port')
- gradient_conductivity: float32 [6, 512, 640], P(None, 'tile', 'port')
The draws below stay inside these ranges and needn't reach their ends.
All inputs are finite; a program needn't handle non-finite values.
Results may differ from the reference program's by a relative error of at most 0.0003.
Values sent between devices are 32-bit elements; how exact they have to be, the bound alone decides.
No kernel may reach another device: no remote copies, remote signals or barrier semaphores. Data moves between devices by JAX's collectives and lax.ppermute only.
A program may use at most 64 MiB of HBM per device.

```python
import math
import jax
import jax.numpy as jnp
from jax import lax

NZ = 6
NY = 640
REGIONS = 8
NX = 512
PORTS = 16


def set_ends(result, key, least, largest):
    longest = result.shape.index(max(result.shape))
    spots = []
    for shift in (0, 1):
        where = [jax.random.randint(jax.random.fold_in(key, axis), (), 0, length) for axis, length in enumerate(result.shape)]
        where[longest] = (where[longest] + shift) % result.shape[longest]
        spots.append(tuple(where))
    return result.at[spots[0]].set(least).at[spots[1]].set(largest)


def shard_levels(key, extent, shards, low, largest):
    factor_of, own = 1.0, jax.random.fold_in(key, 6)
    for position, parts in shards:
        draws = jnp.exp(jax.random.uniform(jax.random.fold_in(own, position), (parts,), jnp.float32, low / len(shards), largest / len(shards)))
        factor_of = factor_of * jnp.repeat(draws, extent[position] // parts).reshape([-1 if axis == position else 1 for axis in range(len(extent))])
    return factor_of


def gaussian(stream_key, extent, scale, most, split=(), kind=jnp.bfloat16):
    array = jax.random.normal(stream_key, extent, jnp.float32) * scale
    if len(split) > 0:
        array = shard_levels(stream_key, extent, split, -0.22, 0.18) * array
    return jnp.clip(array, min=-most, max=most).astype(kind)


def setup_inputs(seed: int = 0) -> dict:
    keys = jax.random.split(jax.random.key(seed), 10)
    electric = gaussian(keys[0], (PORTS, 3, NZ, NX, NY), 1.0, 6.0, ((0, 16), (3, 32)), jnp.float32)
    magnetic = gaussian(keys[1], (PORTS, 3, NZ, NX, NY), 1.0, 6.0, ((0, 16), (3, 32)), jnp.float32)
    adjoint_electric = gaussian(keys[2], (PORTS, 3, NZ, NX, NY), 1.0, 6.0, ((0, 16), (3, 32)), jnp.float32)
    adjoint_magnetic = gaussian(keys[3], (PORTS, 3, NZ, NX, NY), 1.0, 6.0, ((0, 16), (3, 32)), jnp.float32)
    region_labels = set_ends(jax.random.randint(keys[4], (NZ, NX, NY), 0, REGIONS), jax.random.fold_in(keys[4], 1), 0, REGIONS - 1).astype(jnp.int32)
    permittivity_table = jnp.clip(jnp.exp(jax.random.uniform(keys[5], (REGIONS,), jnp.float32, math.log(1.0), math.log(12.0))), 1.0, 12.0)
    conductivity_table = jnp.clip(jnp.exp(jax.random.uniform(keys[6], (REGIONS,), jnp.float32, math.log(0.05), math.log(2.0))), 0.05, 2.0)
    port_cells = set_ends(jax.random.randint(keys[7], (PORTS,), 0, NZ * NX * NY), jax.random.fold_in(keys[7], 1), 0, (NZ * NX * NY) - 1).astype(jnp.int32)
    port_amplitude = gaussian(keys[8], (PORTS, 3), 2.0, 8.0, ((0, 16),), jnp.float32)
    return dict(electric=electric, magnetic=magnetic, adjoint_electric=adjoint_electric, adjoint_magnetic=adjoint_magnetic, region_labels=region_labels, permittivity_table=permittivity_table, conductivity_table=conductivity_table, port_cells=port_cells, port_amplitude=port_amplitude)


TIMESTEP = 0.5
HALF_STEP = 0.25


def step_ahead(values, dimension, beyond):
    following = jnp.concatenate([lax.slice_in_dim(values, 1, values.shape[dimension], axis=dimension), beyond], axis=dimension)
    return following - values


def step_behind(values, dimension, before):
    preceding = jnp.concatenate([before, lax.slice_in_dim(values, 0, values.shape[dimension] - 1, axis=dimension)], axis=dimension)
    return values - preceding


def zero_layer(values, dimension):
    return jnp.zeros_like(lax.slice_in_dim(values, 0, 1, axis=dimension))


def curl_electric(field, next_second, next_third):
    first = step_ahead(field[2], 2, zero_layer(field[2], 2)) - step_ahead(field[1], 0, zero_layer(field[1], 0))
    second = step_ahead(field[0], 0, zero_layer(field[0], 0)) - step_ahead(field[2], 1, next_third)
    third = step_ahead(field[1], 1, next_second) - step_ahead(field[0], 2, zero_layer(field[0], 2))
    return jnp.stack([first, second, third])


def curl_magnetic(field, prev_second, prev_third):
    first = step_behind(field[2], 2, zero_layer(field[2], 2)) - step_behind(field[1], 0, zero_layer(field[1], 0))
    second = step_behind(field[0], 0, zero_layer(field[0], 0)) - step_behind(field[2], 1, prev_third)
    third = step_behind(field[1], 1, prev_second) - step_behind(field[0], 2, zero_layer(field[0], 2))
    return jnp.stack([first, second, third])


def reference(electric, magnetic, adjoint_electric, adjoint_magnetic, region_labels, permittivity_table, conductivity_table, port_cells, port_amplitude):
    permittivity = permittivity_table[region_labels]
    conductivity = conductivity_table[region_labels]
    denominator = permittivity + HALF_STEP * conductivity
    update_gain = (permittivity - HALF_STEP * conductivity) / denominator
    source_gain = TIMESTEP / denominator
    factor = TIMESTEP / (denominator * denominator)
    depth, rows, width = region_labels.shape
    positions = (lax.broadcasted_iota(jnp.int32, (depth, rows, width), 0) * (rows * width)
                 + lax.broadcasted_iota(jnp.int32, (depth, rows, width), 1) * width
                 + lax.broadcasted_iota(jnp.int32, (depth, rows, width), 2))
    zero_x = jnp.zeros((depth, 1, width), jnp.float32)

    def per_port(carry, inputs):
        field, mag_field, adj_field, adj_mag, cell, amplitude = inputs
        forward_magnetic = mag_field - TIMESTEP * curl_electric(field, zero_x, zero_x)
        hits = (positions == cell).astype(jnp.float32)
        source = amplitude[:, None, None, None] * hits[None]
        drive = curl_magnetic(forward_magnetic, zero_x, zero_x) - source
        scaled = source_gain[None] * adj_field
        new_magnetic = adj_mag + curl_electric(scaled, zero_x, zero_x)
        new_electric = update_gain[None] * adj_field - TIMESTEP * curl_magnetic(new_magnetic, zero_x, zero_x)
        corr_a = adj_field[0] * field[0] + adj_field[1] * field[1] + adj_field[2] * field[2]
        corr_b = adj_field[0] * drive[0] + adj_field[1] * drive[1] + adj_field[2] * drive[2]
        term_perm = factor * (conductivity * corr_a - corr_b)
        term_cond = factor * (-permittivity * corr_a - HALF_STEP * corr_b)
        return (carry[0] + term_perm, carry[1] + term_cond), (new_electric, new_magnetic)

    start = (jnp.zeros((depth, rows, width), jnp.float32), jnp.zeros((depth, rows, width), jnp.float32))
    totals, fields = lax.scan(per_port, start, (electric, magnetic, adjoint_electric, adjoint_magnetic, port_cells, port_amplitude))
    return fields[0], fields[1], totals[0], totals[1]
```

```python
import jax
import jax.numpy as jnp
from jax import lax
from jax.sharding import PartitionSpec as P

TIMESTEP = 0.5
HALF_STEP = 0.25
PLANES = 3


def from_behind(value, axis, steps):
    count = lax.axis_size(axis)
    first, last = (max(0, -steps), min(count, count - steps))
    return lax.ppermute(value, axis, [(source, source + steps) for source in range(first, last)])


def step_ahead(values, dimension, beyond):
    following = jnp.concatenate(
        [lax.slice_in_dim(values, 1, values.shape[dimension], axis=dimension), beyond],
        axis=dimension,
    )
    return following - values


def step_behind(values, dimension, before):
    preceding = jnp.concatenate(
        [before, lax.slice_in_dim(values, 0, values.shape[dimension] - 1, axis=dimension)],
        axis=dimension,
    )
    return values - preceding


def zero_layer(values, dimension):
    return jnp.zeros_like(lax.slice_in_dim(values, 0, 1, axis=dimension))


def curl_electric(field, next_second, next_third):
    first = step_ahead(field[2], 2, zero_layer(field[2], 2)) - step_ahead(
        field[1], 0, zero_layer(field[1], 0)
    )
    second = step_ahead(field[0], 0, zero_layer(field[0], 0)) - step_ahead(field[2], 1, next_third)
    third = step_ahead(field[1], 1, next_second) - step_ahead(field[0], 2, zero_layer(field[0], 2))
    return jnp.stack([first, second, third])


def curl_magnetic(field, prev_second, prev_third):
    first = step_behind(field[2], 2, zero_layer(field[2], 2)) - step_behind(
        field[1], 0, zero_layer(field[1], 0)
    )
    second = step_behind(field[0], 0, zero_layer(field[0], 0)) - step_behind(
        field[2], 1, prev_third
    )
    third = step_behind(field[1], 1, prev_second) - step_behind(
        field[0], 2, zero_layer(field[0], 2)
    )
    return jnp.stack([first, second, third])


def on_device(
    electric,
    magnetic,
    adjoint_electric,
    adjoint_magnetic,
    region_labels,
    permittivity_table,
    conductivity_table,
    port_cells,
    port_amplitude,
):
    field = electric[0]
    mag_field = magnetic[0]
    adj_field = adjoint_electric[0]
    adj_mag = adjoint_magnetic[0]
    depth, columns, width = region_labels.shape
    tile_index = lax.axis_index("tile")
    offset = tile_index * columns
    total_rows = columns * lax.axis_size("tile")
    corr_a = adj_field[0] * field[0] + adj_field[1] * field[1] + adj_field[2] * field[2]
    permittivity = jnp.zeros((depth, columns, width), jnp.float32)
    conductivity = jnp.zeros((depth, columns, width), jnp.float32)
    for region in range(permittivity_table.shape[0]):
        matches = region_labels == region
        permittivity = jnp.where(matches, permittivity_table[region], permittivity)
        conductivity = jnp.where(matches, conductivity_table[region], conductivity)
    denominator = permittivity + HALF_STEP * conductivity
    update_gain = (permittivity - HALF_STEP * conductivity) / denominator
    source_gain = TIMESTEP / denominator
    scaled = source_gain[None] * adj_field
    upper = from_behind((field[1:3, :, 0:1, :], scaled[1:3, :, 0:1, :]), "tile", -1)
    field_next, scaled_next = upper
    forward_magnetic = mag_field - TIMESTEP * curl_electric(field, field_next[0], field_next[1])
    new_magnetic = adj_mag + curl_electric(scaled, scaled_next[0], scaled_next[1])
    forward_rim, adjoint_rim = from_behind(
        (forward_magnetic[1:3, :, -1:, :], new_magnetic[1:3, :, -1:, :]), "tile", 1
    )
    positions = (
        lax.broadcasted_iota(jnp.int32, (depth, columns, width), 0) * (total_rows * width)
        + (lax.broadcasted_iota(jnp.int32, (depth, columns, width), 1) + offset) * width
        + lax.broadcasted_iota(jnp.int32, (depth, columns, width), 2)
    )
    hits = (positions == port_cells[0]).astype(jnp.float32)
    source = port_amplitude[0][:, None, None, None] * hits[None]
    drive = curl_magnetic(forward_magnetic, forward_rim[0], forward_rim[1]) - source
    corr_b = adj_field[0] * drive[0] + adj_field[1] * drive[1] + adj_field[2] * drive[2]
    ports = lax.axis_size("port")
    share = width // ports
    groups = depth // PLANES
    packed = jnp.stack([corr_a, corr_b]).reshape(2, groups, PLANES, columns, ports, share)
    packed = packed.transpose(4, 0, 1, 3, 2, 5).reshape(ports, 2 * groups, columns, PLANES * share)
    gathered = lax.all_to_all(packed, "port", 0, 0, tiled=True)
    summed = jnp.sum(gathered, axis=0).reshape(2, groups, columns, PLANES, share)
    summed_a, summed_b = summed.transpose(0, 1, 3, 2, 4).reshape(2, depth, columns, share)
    new_electric = update_gain[None] * adj_field - TIMESTEP * curl_magnetic(
        new_magnetic, adjoint_rim[0], adjoint_rim[1]
    )
    begin = lax.axis_index("port") * share
    perm_share = lax.dynamic_slice_in_dim(permittivity, begin, share, 2)
    cond_share = lax.dynamic_slice_in_dim(conductivity, begin, share, 2)
    denom_share = perm_share + HALF_STEP * cond_share
    factor = TIMESTEP / (denom_share * denom_share)
    gradient_perm = factor * (cond_share * summed_a - summed_b)
    gradient_cond = factor * (-perm_share * summed_a - HALF_STEP * summed_b)
    return (new_electric[None], new_magnetic[None], gradient_perm, gradient_cond)


def solution(mesh):
    return jax.shard_map(
        on_device,
        mesh=mesh,
        in_specs=(
            P("port", None, None, "tile", None),
            P("port", None, None, "tile", None),
            P("port", None, None, "tile", None),
            P("port", None, None, "tile", None),
            P(None, "tile", None),
            P(),
            P(),
            P("port"),
            P("port", None),
        ),
        out_specs=(
            P("port", None, None, "tile", None),
            P("port", None, None, "tile", None),
            P(None, "tile", "port"),
            P(None, "tile", "port"),
        ),
        check_vma=False,
    )
```

```python
import functools

import jax
import jax.numpy as jnp
from jax import lax
from jax.experimental import pallas as pl
from jax.experimental.pallas import tpu as pltpu
from jax.sharding import PartitionSpec as P

TIMESTEP = 0.5
HALF_STEP = 0.25
PLANES = 3
LANES = 128
VMEM = pltpu.VMEM
SMEM = pltpu.SMEM


def from_behind(value, axis, steps):
    count = lax.axis_size(axis)
    first, last = (max(0, -steps), min(count, count - steps))
    return lax.ppermute(value, axis, [(source, source + steps) for source in range(first, last)])


def lane_iota(shape):
    return lax.broadcasted_iota(jnp.int32, shape, len(shape) - 1)


def row_iota(shape):
    return lax.broadcasted_iota(jnp.int32, shape, len(shape) - 2)


def lane_next(value):
    width = value.shape[1]
    return jnp.where(lane_iota(value.shape) == width - 1, 0.0, pltpu.roll(value, width - 1, 1))


def lane_prev(value):
    return jnp.where(lane_iota(value.shape) == 0, 0.0, pltpu.roll(value, 1, 1))


def row_next(value, beyond):
    rows = value.shape[0]
    return jnp.where(row_iota(value.shape) == rows - 1, beyond, pltpu.roll(value, rows - 1, 0))


def row_prev(value, before):
    return jnp.where(row_iota(value.shape) == 0, before, pltpu.roll(value, 1, 0))


def look_up(labels, entries):
    count = len(entries)
    level = list(entries)
    bit = 1
    while len(level) > 1:
        odd = (labels & bit) != 0
        level = [
            jnp.where(odd, level[i + 1], level[i]) if i + 1 < len(level) else level[i]
            for i in range(0, len(level), 2)
        ]
        bit *= 2
    assert count <= bit
    return level[0]


def region_values(perm_ref, cond_ref):
    shape = (1, LANES)
    perm = [jnp.full(shape, perm_ref[r], jnp.float32) for r in range(perm_ref.shape[0])]
    cond = [jnp.full(shape, cond_ref[r], jnp.float32) for r in range(cond_ref.shape[0])]
    return perm, cond


def widen(entries, width):
    return [jnp.concatenate([entry] * (width // LANES), axis=1) for entry in entries]


def gains(perm_ref, cond_ref, width):
    perm, cond = region_values(perm_ref, cond_ref)
    denominator = [p + HALF_STEP * c for p, c in zip(perm, cond, strict=True)]
    source = [TIMESTEP / d for d in denominator]
    update = [(p - HALF_STEP * c) / d for p, c, d in zip(perm, cond, denominator, strict=True)]
    return widen(source, width), widen(update, width)


def edge_kernel(e, m, ae, am, labels, perm, cond, up, down):
    depth, rows, width = labels.shape
    source, _ = gains(perm, cond, width)
    last = rows - 1

    def row(ref, c, z, r):
        if z == depth:
            return jnp.zeros((1, width), jnp.float32)
        return ref[0, c, z, r : r + 1, :]

    scaled = []
    for z in range(depth):
        gain = look_up(labels[z, last : last + 1, :], source)
        scaled.append([gain * row(ae, c, z, last) for c in range(3)])
    scaled.append([jnp.zeros((1, width), jnp.float32)] * 3)
    for z in range(depth):
        ex, ey, ez = (row(e, c, z, last) for c in range(3))
        sx, sy, sz = scaled[z]
        up[z : z + 1, :] = row(m, 1, z, last) - TIMESTEP * ((row(e, 0, z + 1, last) - ex) + ez)
        up[depth + z : depth + z + 1, :] = row(m, 2, z, last) + TIMESTEP * (ey + (lane_next(ex) - ex))
        up[2 * depth + z : 2 * depth + z + 1, :] = row(am, 1, z, last) + ((scaled[z + 1][0] - sx) + sz)
        up[3 * depth + z : 3 * depth + z + 1, :] = row(am, 2, z, last) - (sy + (lane_next(sx) - sx))
        gain = look_up(labels[z, 0:1, :], source)
        down[z : z + 1, :] = row(e, 1, z, 0)
        down[depth + z : depth + z + 1, :] = row(e, 2, z, 0)
        down[2 * depth + z : 2 * depth + z + 1, :] = gain * row(ae, 1, z, 0)
        down[3 * depth + z : 3 * depth + z + 1, :] = gain * row(ae, 2, z, 0)


def pack(planes, share, ports):
    rows = planes[0].shape[0]
    lane = lane_iota((rows, LANES))
    blocks = []
    for port in range(ports):
        tile, offset = divmod(port * share, LANES)
        pieces = []
        for j, plane in enumerate(planes):
            piece = plane[:, tile * LANES : (tile + 1) * LANES]
            if offset + share > LANES:
                piece = jnp.where(
                    lane >= offset, piece, plane[:, (tile + 1) * LANES : (tile + 2) * LANES]
                )
            shift = (j * share - offset) % LANES
            pieces.append(pltpu.roll(piece, shift, 1) if shift else piece)
        block = pieces[-1]
        for j in range(len(planes) - 2, -1, -1):
            block = jnp.where(lane < (j + 1) * share, pieces[j], block)
        blocks.append(block)
    return blocks


def correlation_kernel(ports, e, m, ae, above, below, cells, amplitude, packed):
    _, _, depth, rows, width = e.shape
    share = width // ports
    tile = lax.axis_index("tile")
    plane_cells = lax.axis_size("tile") * rows * width
    target = cells[0] - tile * (rows * width)
    inside = jnp.where(tile > 0, 1.0, 0.0)
    position = row_iota((rows, width)) * width + lane_iota((rows, width))

    def at(ref, c, z):
        return ref[0, c, z] if z < depth else jnp.zeros((rows, width), jnp.float32)

    zero = jnp.zeros((rows, width), jnp.float32)
    fx_prev, fy_prev = zero, zero
    sums_a, sums_b = [], []
    for z in range(depth):
        ex, ey, ez = (at(e, c, z) for c in range(3))
        next_y, next_z = below[z : z + 1, :], below[depth + z : depth + z + 1, :]
        fx = at(m, 0, z) - TIMESTEP * ((lane_next(ez) - ez) - (at(e, 1, z + 1) - ey))
        fy = at(m, 1, z) - TIMESTEP * ((at(e, 0, z + 1) - ex) - (row_next(ez, next_z) - ez))
        fz = at(m, 2, z) - TIMESTEP * ((row_next(ey, next_y) - ey) - (lane_next(ex) - ex))
        prev_y = inside * (above[z : z + 1, :] + TIMESTEP * ez[0:1])
        prev_z = inside * (above[depth + z : depth + z + 1, :] - TIMESTEP * ey[0:1])
        hit = position == target - z * plane_cells
        drive_x = ((fz - lane_prev(fz)) - (fy - fy_prev)) - jnp.where(hit, amplitude[0, 0], 0.0)
        drive_y = ((fx - fx_prev) - (fz - row_prev(fz, prev_z))) - jnp.where(hit, amplitude[0, 1], 0.0)
        drive_z = ((fy - row_prev(fy, prev_y)) - (fx - lane_prev(fx))) - jnp.where(
            hit, amplitude[0, 2], 0.0
        )
        ax, ay, az = (at(ae, c, z) for c in range(3))
        sums_a.append(ax * ex + ay * ey + az * ez)
        sums_b.append(ax * drive_x + ay * drive_y + az * drive_z)
        fx_prev, fy_prev = fx, fy
        if z % PLANES == PLANES - 1:
            group = z // PLANES
            for f, sums in enumerate((sums_a, sums_b)):
                for port, block in enumerate(pack(sums, share, ports)):
                    packed[port, f * (depth // PLANES) + group] = block
            sums_a, sums_b = [], []


def field_kernel(ae, am, labels, above, below, perm, cond, new_e, new_m):
    depth, rows, width = labels.shape
    source, update = gains(perm, cond, width)
    inside = jnp.where(lax.axis_index("tile") > 0, 1.0, 0.0)
    zero = jnp.zeros((rows, width), jnp.float32)

    def scaled(z):
        if z == depth:
            return [zero] * 3
        gain = look_up(labels[z], source)
        return [gain * ae[0, c, z] for c in range(3)]

    nx_prev, ny_prev = zero, zero
    here = scaled(0)
    for z in range(depth):
        after = scaled(z + 1)
        sx, sy, sz = here
        next_y = below[2 * depth + z : 2 * depth + z + 1, :]
        next_z = below[3 * depth + z : 3 * depth + z + 1, :]
        nx = am[0, 0, z] + ((lane_next(sz) - sz) - (after[1] - sy))
        ny = am[0, 1, z] + ((after[0] - sx) - (row_next(sz, next_z) - sz))
        nz = am[0, 2, z] + ((row_next(sy, next_y) - sy) - (lane_next(sx) - sx))
        prev_y = inside * (above[2 * depth + z : 2 * depth + z + 1, :] - sz[0:1])
        prev_z = inside * (above[3 * depth + z : 3 * depth + z + 1, :] + sy[0:1])
        new_m[0, 0, z] = nx
        new_m[0, 1, z] = ny
        new_m[0, 2, z] = nz
        gain = look_up(labels[z], update)
        new_e[0, 0, z] = gain * ae[0, 0, z] - TIMESTEP * ((nz - lane_prev(nz)) - (ny - ny_prev))
        new_e[0, 1, z] = gain * ae[0, 1, z] - TIMESTEP * ((nx - nx_prev) - (nz - row_prev(nz, prev_z)))
        new_e[0, 2, z] = gain * ae[0, 2, z] - TIMESTEP * ((ny - row_prev(ny, prev_y)) - (nx - lane_prev(nx)))
        nx_prev, ny_prev = nx, ny
        here = after


def gradient_kernel(gathered, labels, perm, cond, grad_perm, grad_cond):
    ports, slabs, rows, _ = gathered.shape
    depth, _, share = grad_perm.shape
    width = labels.shape[2]
    groups = depth // PLANES
    begin = lax.axis_index("port") * share
    perms, conds = region_values(perm, cond)
    denominators = [p + HALF_STEP * c for p, c in zip(perms, conds, strict=True)]
    factors = [TIMESTEP / (d * d) for d in denominators]
    sums = []
    for slab in range(slabs):
        total = gathered[0, slab]
        for port in range(1, ports):
            total = total + gathered[port, slab]
        sums.append(total)
    for z in range(depth):
        group, j = divmod(z, PLANES)
        corr_a, corr_b = (
            pltpu.roll(sums[f * groups + group], (LANES - j * share) % LANES, 1) if j else sums[f * groups + group]
            for f in range(2)
        )
        mine = pltpu.roll(labels[z], lax.rem(width - begin, width), 1)[:, :LANES]
        factor = look_up(mine, factors)
        permittivity = look_up(mine, perms)
        conductivity = look_up(mine, conds)
        by_perm = factor * (conductivity * corr_a - corr_b)
        by_cond = factor * (-permittivity * corr_a - HALF_STEP * corr_b)
        grad_perm[z] = by_perm[:, :share]
        grad_cond[z] = by_cond[:, :share]


def spec(space):
    return pl.BlockSpec(memory_space=space)


def call(kernel, inputs, spaces, outs, flops, moved):
    return pl.pallas_call(
        kernel,
        out_shape=outs,
        in_specs=[spec(space) for space in spaces],
        out_specs=jax.tree.map(lambda _: spec(VMEM), outs),
        cost_estimate=pl.CostEstimate(flops=flops, bytes_accessed=moved, transcendentals=0),
    )(*inputs)


def on_device(
    electric,
    magnetic,
    adjoint_electric,
    adjoint_magnetic,
    region_labels,
    permittivity_table,
    conductivity_table,
    port_cells,
    port_amplitude,
):
    depth, rows, width = region_labels.shape
    ports = lax.axis_size("port")
    share = width // ports
    cells = depth * rows * width

    def array(*shape):
        return jax.ShapeDtypeStruct(shape, jnp.float32)

    edge = array(4 * depth, width)
    up, down = call(
        edge_kernel,
        (electric, magnetic, adjoint_electric, adjoint_magnetic, region_labels, permittivity_table, conductivity_table),
        (VMEM,) * 5 + (SMEM,) * 2,
        (edge, edge),
        10 * cells,
        cells * 4,
    )
    below = from_behind(down, "tile", -1)
    above = from_behind(up, "tile", 1)
    packed = call(
        functools.partial(correlation_kernel, ports),
        (electric, magnetic, adjoint_electric, above, below, port_cells, port_amplitude),
        (VMEM,) * 5 + (SMEM,) * 2,
        array(ports, 2 * depth // PLANES, rows, LANES),
        60 * cells,
        cells * 4 * 11,
    )
    gathered = lax.all_to_all(packed, "port", 0, 0, tiled=True)
    new_electric, new_magnetic = call(
        field_kernel,
        (adjoint_electric, adjoint_magnetic, region_labels, above, below, permittivity_table, conductivity_table),
        (VMEM,) * 5 + (SMEM,) * 2,
        (array(1, 3, depth, rows, width), array(1, 3, depth, rows, width)),
        80 * cells,
        cells * 4 * 13,
    )
    gradient = array(depth, rows, share)
    gradient_perm, gradient_cond = call(
        gradient_kernel,
        (gathered, region_labels, permittivity_table, conductivity_table),
        (VMEM,) * 2 + (SMEM,) * 2,
        (gradient, gradient),
        4 * cells,
        cells * 4 * 3,
    )
    return (new_electric, new_magnetic, gradient_perm, gradient_cond)


def solution(mesh):
    return jax.shard_map(
        on_device,
        mesh=mesh,
        in_specs=(
            P("port", None, None, "tile", None),
            P("port", None, None, "tile", None),
            P("port", None, None, "tile", None),
            P("port", None, None, "tile", None),
            P(None, "tile", None),
            P(),
            P(),
            P("port"),
            P("port", None),
        ),
        out_specs=(
            P("port", None, None, "tile", None),
            P("port", None, None, "tile", None),
            P(None, "tile", "port"),
            P(None, "tile", "port"),
        ),
        check_vma=False,
    )
```

```python
import functools

import jax
import jax.numpy as jnp
from jax import lax
from jax.experimental import pallas as pl
from jax.experimental.pallas import tpu as pltpu
from jax.sharding import PartitionSpec as P

TIMESTEP = 0.5
HALF_STEP = 0.25
PLANES = 3
LANES = 128
VMEM = pltpu.VMEM
SMEM = pltpu.SMEM
ANY = pl.ANY
HBM_BLOCK = None


def swap(value, axis, first):
    pairs = range(first, lax.axis_size(axis) - 1, 2)
    return lax.ppermute(value, axis, [(i, i + 1) for i in pairs] + [(i + 1, i) for i in pairs])


def lane_iota(shape):
    return lax.broadcasted_iota(jnp.int32, shape, len(shape) - 1)


def row_iota(shape):
    return lax.broadcasted_iota(jnp.int32, shape, len(shape) - 2)


def lane_next(value):
    width = value.shape[1]
    return jnp.where(lane_iota(value.shape) == width - 1, 0.0, pltpu.roll(value, width - 1, 1))


def lane_prev(value):
    return jnp.where(lane_iota(value.shape) == 0, 0.0, pltpu.roll(value, 1, 1))


def row_next(value, beyond):
    rows = value.shape[0]
    return jnp.where(row_iota(value.shape) == rows - 1, beyond, pltpu.roll(value, rows - 1, 0))


def row_prev(value, before):
    return jnp.where(row_iota(value.shape) == 0, before, pltpu.roll(value, 1, 0))


def look_up(labels, entries):
    count = len(entries)
    level = list(entries)
    bit = 1
    while len(level) > 1:
        odd = (labels & bit) != 0
        level = [
            jnp.where(odd, level[i + 1], level[i]) if i + 1 < len(level) else level[i]
            for i in range(0, len(level), 2)
        ]
        bit *= 2
    assert count <= bit
    return level[0]


def region_values(perm_ref, cond_ref):
    shape = (1, LANES)
    perm = [jnp.full(shape, perm_ref[r], jnp.float32) for r in range(perm_ref.shape[0])]
    cond = [jnp.full(shape, cond_ref[r], jnp.float32) for r in range(cond_ref.shape[0])]
    return perm, cond


def widen(entries, width):
    return [jnp.concatenate([entry] * (width // LANES), axis=1) for entry in entries]


def gains(perm_ref, cond_ref, width):
    perm, cond = region_values(perm_ref, cond_ref)
    denominator = [p + HALF_STEP * c for p, c in zip(perm, cond, strict=True)]
    source = [TIMESTEP / d for d in denominator]
    update = [(p - HALF_STEP * c) / d for p, c, d in zip(perm, cond, denominator, strict=True)]
    return widen(source, width), widen(update, width)


def edge_kernel(e, m, ae, am, labels, perm, cond, near, far, e_last, m_last, ae_last, am_last, e_first, ae_first, marks, sems):
    _, _, depth, rows, width = e.shape
    last = rows - 1
    moves = (
        (ae.at[0, :, :, pl.ds(last, 1)], ae_last),
        (ae.at[0, pl.ds(1, 2), :, pl.ds(0, 1)], ae_first),
        (labels.at[:, pl.ds(last, 1)], marks.at[0]),
        (labels.at[:, pl.ds(0, 1)], marks.at[1]),
        (e.at[0, :, :, pl.ds(last, 1)], e_last),
        (e.at[0, pl.ds(1, 2), :, pl.ds(0, 1)], e_first),
        (m.at[0, pl.ds(1, 2), :, pl.ds(last, 1)], m_last),
        (am.at[0, pl.ds(1, 2), :, pl.ds(last, 1)], am_last),
    )
    copies = [pltpu.make_async_copy(src, dst, sems.at[i]) for i, (src, dst) in enumerate(moves)]
    for copy in copies:
        copy.start()
    source, _ = gains(perm, cond, width)
    odd = lax.rem(lax.axis_index("tile"), 2) == 1
    for copy in copies:
        copy.wait()
    zero = jnp.zeros((1, width), jnp.float32)

    def row(ref, c, z):
        return ref[c, z] if z < depth else zero

    scaled = []
    for z in range(depth):
        gain = look_up(marks[0, z], source)
        scaled.append([gain * row(ae_last, c, z) for c in range(3)])
    scaled.append([zero] * 3)
    for z in range(depth):
        ex, ey, ez = (row(e_last, c, z) for c in range(3))
        sx, sy, sz = scaled[z]
        gain = look_up(marks[1, z], source)
        up = (
            m_last[0, z] - TIMESTEP * ((row(e_last, 0, z + 1) - ex) + ez),
            m_last[1, z] + TIMESTEP * (ey + (lane_next(ex) - ex)),
            am_last[0, z] + ((scaled[z + 1][0] - sx) + sz),
            am_last[1, z] - (sy + (lane_next(sx) - sx)),
        )
        down = (e_first[0, z], e_first[1, z], gain * ae_first[0, z], gain * ae_first[1, z])
        for i, (above, below) in enumerate(zip(up, down, strict=True)):
            at = i * depth + z
            near[at : at + 1, :] = jnp.where(odd, below, above)
            far[at : at + 1, :] = jnp.where(odd, above, below)


def from_tiles(near, far):
    odd = lax.rem(lax.axis_index("tile"), 2) == 1

    def above(i):
        return jnp.where(odd, near[i : i + 1, :], far[i : i + 1, :])

    def below(i):
        return jnp.where(odd, far[i : i + 1, :], near[i : i + 1, :])

    return above, below


def pack(planes, share, ports):
    rows = planes[0].shape[0]
    lane = lane_iota((rows, LANES))
    blocks = []
    for port in range(ports):
        tile, offset = divmod(port * share, LANES)
        pieces = []
        for j, plane in enumerate(planes):
            piece = plane[:, tile * LANES : (tile + 1) * LANES]
            if offset + share > LANES:
                piece = jnp.where(
                    lane >= offset, piece, plane[:, (tile + 1) * LANES : (tile + 2) * LANES]
                )
            shift = (j * share - offset) % LANES
            pieces.append(pltpu.roll(piece, shift, 1) if shift else piece)
        block = pieces[-1]
        for j in range(len(planes) - 2, -1, -1):
            block = jnp.where(lane < (j + 1) * share, pieces[j], block)
        blocks.append(block)
    return blocks


def correlation_kernel(ports, e, m, ae, near, far, cells, amplitude, packed):
    _, _, depth, rows, width = e.shape
    share = width // ports
    tile = lax.axis_index("tile")
    above, below = from_tiles(near, far)
    plane_cells = lax.axis_size("tile") * rows * width
    target = cells[0] - tile * (rows * width)
    inside = jnp.where(tile > 0, 1.0, 0.0)
    position = row_iota((rows, width)) * width + lane_iota((rows, width))

    def at(ref, c, z):
        return ref[0, c, z] if z < depth else jnp.zeros((rows, width), jnp.float32)

    zero = jnp.zeros((rows, width), jnp.float32)
    fx_prev, fy_prev = zero, zero
    sums_a, sums_b = [], []
    for z in range(depth):
        ex, ey, ez = (at(e, c, z) for c in range(3))
        next_y, next_z = below(z), below(depth + z)
        fx = at(m, 0, z) - TIMESTEP * ((lane_next(ez) - ez) - (at(e, 1, z + 1) - ey))
        fy = at(m, 1, z) - TIMESTEP * ((at(e, 0, z + 1) - ex) - (row_next(ez, next_z) - ez))
        fz = at(m, 2, z) - TIMESTEP * ((row_next(ey, next_y) - ey) - (lane_next(ex) - ex))
        prev_y = inside * (above(z) + TIMESTEP * ez[0:1])
        prev_z = inside * (above(depth + z) - TIMESTEP * ey[0:1])
        hit = position == target - z * plane_cells
        drive_x = ((fz - lane_prev(fz)) - (fy - fy_prev)) - jnp.where(hit, amplitude[0, 0], 0.0)
        drive_y = ((fx - fx_prev) - (fz - row_prev(fz, prev_z))) - jnp.where(hit, amplitude[0, 1], 0.0)
        drive_z = ((fy - row_prev(fy, prev_y)) - (fx - lane_prev(fx))) - jnp.where(
            hit, amplitude[0, 2], 0.0
        )
        ax, ay, az = (at(ae, c, z) for c in range(3))
        sums_a.append(ax * ex + ay * ey + az * ez)
        sums_b.append(ax * drive_x + ay * drive_y + az * drive_z)
        fx_prev, fy_prev = fx, fy
        if z % PLANES == PLANES - 1:
            group = z // PLANES
            for f, sums in enumerate((sums_a, sums_b)):
                for port, block in enumerate(pack(sums, share, ports)):
                    packed[port, f * (depth // PLANES) + group] = block
            sums_a, sums_b = [], []


def field_kernel(ae, am, labels, near, far, perm, cond, new_e, new_m):
    depth, rows, width = labels.shape
    source, update = gains(perm, cond, width)
    above, below = from_tiles(near, far)
    inside = jnp.where(lax.axis_index("tile") > 0, 1.0, 0.0)
    zero = jnp.zeros((rows, width), jnp.float32)

    def scaled(z):
        if z == depth:
            return [zero] * 3
        gain = look_up(labels[z], source)
        return [gain * ae[0, c, z] for c in range(3)]

    nx_prev, ny_prev = zero, zero
    here = scaled(0)
    for z in range(depth):
        after = scaled(z + 1)
        sx, sy, sz = here
        next_y = below(2 * depth + z)
        next_z = below(3 * depth + z)
        nx = am[0, 0, z] + ((lane_next(sz) - sz) - (after[1] - sy))
        ny = am[0, 1, z] + ((after[0] - sx) - (row_next(sz, next_z) - sz))
        nz = am[0, 2, z] + ((row_next(sy, next_y) - sy) - (lane_next(sx) - sx))
        prev_y = inside * (above(2 * depth + z) - sz[0:1])
        prev_z = inside * (above(3 * depth + z) + sy[0:1])
        new_m[0, 0, z] = nx
        new_m[0, 1, z] = ny
        new_m[0, 2, z] = nz
        gain = look_up(labels[z], update)
        new_e[0, 0, z] = gain * ae[0, 0, z] - TIMESTEP * ((nz - lane_prev(nz)) - (ny - ny_prev))
        new_e[0, 1, z] = gain * ae[0, 1, z] - TIMESTEP * ((nx - nx_prev) - (nz - row_prev(nz, prev_z)))
        new_e[0, 2, z] = gain * ae[0, 2, z] - TIMESTEP * ((ny - row_prev(ny, prev_y)) - (nx - lane_prev(nx)))
        nx_prev, ny_prev = nx, ny
        here = after


def gradient_kernel(gathered, labels, perm, cond, grad_perm, grad_cond):
    ports, slabs, rows, _ = gathered.shape
    depth, _, share = grad_perm.shape
    width = labels.shape[2]
    groups = depth // PLANES
    begin = lax.axis_index("port") * share
    perms, conds = region_values(perm, cond)
    denominators = [p + HALF_STEP * c for p, c in zip(perms, conds, strict=True)]
    factors = [TIMESTEP / (d * d) for d in denominators]
    sums = []
    for slab in range(slabs):
        total = gathered[0, slab]
        for port in range(1, ports):
            total = total + gathered[port, slab]
        sums.append(total)
    for z in range(depth):
        group, j = divmod(z, PLANES)
        corr_a, corr_b = (
            pltpu.roll(sums[f * groups + group], (LANES - j * share) % LANES, 1) if j else sums[f * groups + group]
            for f in range(2)
        )
        mine = pltpu.roll(labels[z], lax.rem(width - begin, width), 1)[:, :LANES]
        factor = look_up(mine, factors)
        permittivity = look_up(mine, perms)
        conductivity = look_up(mine, conds)
        by_perm = factor * (conductivity * corr_a - corr_b)
        by_cond = factor * (-permittivity * corr_a - HALF_STEP * corr_b)
        grad_perm[z] = by_perm[:, :share]
        grad_cond[z] = by_cond[:, :share]


def call(kernel, inputs, spaces, outs, out_spaces, flops, moved, scratch=()):
    inputs = [pltpu.with_memory_space_constraint(x, VMEM) if space is VMEM else x for x, space in zip(inputs, spaces, strict=True)]
    return pl.pallas_call(
        kernel,
        out_shape=tuple(space(out.shape, out.dtype) if space is VMEM else out for out, space in zip(outs, out_spaces, strict=True)),
        in_specs=[pl.BlockSpec(memory_space=VMEM if space is HBM_BLOCK else space) for space in spaces],
        out_specs=tuple(pl.BlockSpec(memory_space=VMEM) for _ in outs),
        scratch_shapes=scratch,
        cost_estimate=pl.CostEstimate(flops=flops, bytes_accessed=moved, transcendentals=0),
    )(*inputs)


def on_device(
    electric,
    magnetic,
    adjoint_electric,
    adjoint_magnetic,
    region_labels,
    permittivity_table,
    conductivity_table,
    port_cells,
    port_amplitude,
):
    depth, rows, width = region_labels.shape
    ports = lax.axis_size("port")
    share = width // ports
    cells = depth * rows * width

    def array(*shape):
        return jax.ShapeDtypeStruct(shape, jnp.float32)

    edge = array(4 * depth, width)
    near, far = call(
        edge_kernel,
        (electric, magnetic, adjoint_electric, adjoint_magnetic, region_labels, permittivity_table, conductivity_table),
        (ANY,) * 5 + (SMEM,) * 2,
        (edge, edge),
        (VMEM, VMEM),
        10 * cells,
        cells * 4,
        [
            VMEM((count, depth, 1, width), jnp.float32) for count in (3, 2, 3, 2, 2, 2)
        ] + [VMEM((2, depth, 1, width), jnp.int32), pltpu.SemaphoreType.DMA((8,))],
    )
    near, far = swap(near, "tile", 0), swap(far, "tile", 1)
    (packed,) = call(
        functools.partial(correlation_kernel, ports),
        (electric, magnetic, adjoint_electric, near, far, port_cells, port_amplitude),
        (VMEM,) * 5 + (SMEM,) * 2,
        (array(ports, 2 * depth // PLANES, rows, LANES),),
        (VMEM,),
        60 * cells,
        cells * 4 * 11,
    )
    gathered = lax.all_to_all(packed, "port", 0, 0, tiled=True)
    new_electric, new_magnetic = call(
        field_kernel,
        (adjoint_electric, adjoint_magnetic, region_labels, near, far, permittivity_table, conductivity_table),
        (VMEM, HBM_BLOCK, HBM_BLOCK, VMEM, VMEM) + (SMEM,) * 2,
        (array(1, 3, depth, rows, width), array(1, 3, depth, rows, width)),
        (HBM_BLOCK,) * 2,
        80 * cells,
        cells * 4 * 13,
    )
    gradient = array(depth, rows, share)
    gradient_perm, gradient_cond = call(
        gradient_kernel,
        (gathered, region_labels, permittivity_table, conductivity_table),
        (VMEM,) * 2 + (SMEM,) * 2,
        (gradient, gradient),
        (HBM_BLOCK,) * 2,
        4 * cells,
        cells * 4 * 3,
    )
    return (new_electric, new_magnetic, gradient_perm, gradient_cond)


def solution(mesh):
    return jax.shard_map(
        on_device,
        mesh=mesh,
        in_specs=(
            P("port", None, None, "tile", None),
            P("port", None, None, "tile", None),
            P("port", None, None, "tile", None),
            P("port", None, None, "tile", None),
            P(None, "tile", None),
            P(),
            P(),
            P("port"),
            P("port", None),
        ),
        out_specs=(
            P("port", None, None, "tile", None),
            P("port", None, None, "tile", None),
            P(None, "tile", "port"),
            P(None, "tile", "port"),
        ),
        check_vma=False,
    )
```

```python
import functools

import jax
import jax.numpy as jnp
from jax import lax
from jax.experimental import pallas as pl
from jax.experimental.pallas import tpu as pltpu
from jax.sharding import PartitionSpec as P

TIMESTEP = 0.5
HALF_STEP = 0.25
PLANES = 3
LANES = 128
EDGE = 8
VMEM_LIMIT = 12 << 20
VMEM = pltpu.VMEM
SMEM = pltpu.SMEM
HBM = pltpu.HBM
HBM_BLOCK = None


def swap(value, axis, first):
    pairs = range(first, lax.axis_size(axis) - 1, 2)
    return lax.ppermute(value, axis, [(i, i + 1) for i in pairs] + [(i + 1, i) for i in pairs])


def lane_iota(shape):
    return lax.broadcasted_iota(jnp.int32, shape, len(shape) - 1)


def row_iota(shape):
    return lax.broadcasted_iota(jnp.int32, shape, len(shape) - 2)


def lane_next(value):
    width = value.shape[1]
    return jnp.where(lane_iota(value.shape) == width - 1, 0.0, pltpu.roll(value, width - 1, 1))


def lane_prev(value):
    return jnp.where(lane_iota(value.shape) == 0, 0.0, pltpu.roll(value, 1, 1))


def row_next(value, beyond):
    rows = value.shape[0]
    return jnp.where(row_iota(value.shape) == rows - 1, beyond, pltpu.roll(value, rows - 1, 0))


def row_prev(value, before):
    return jnp.where(row_iota(value.shape) == 0, before, pltpu.roll(value, 1, 0))


def look_up(labels, entries):
    count = len(entries)
    level = list(entries)
    bit = 1
    while len(level) > 1:
        odd = (labels & bit) != 0
        level = [
            jnp.where(odd, level[i + 1], level[i]) if i + 1 < len(level) else level[i]
            for i in range(0, len(level), 2)
        ]
        bit *= 2
    assert count <= bit
    return level[0]


def region_values(perm_ref, cond_ref):
    shape = (1, LANES)
    perm = [jnp.full(shape, perm_ref[r], jnp.float32) for r in range(perm_ref.shape[0])]
    cond = [jnp.full(shape, cond_ref[r], jnp.float32) for r in range(cond_ref.shape[0])]
    return perm, cond


def widen(entries, width):
    return [jnp.concatenate([entry] * (width // LANES), axis=1) for entry in entries]


def gains(perm_ref, cond_ref, width):
    perm, cond = region_values(perm_ref, cond_ref)
    denominator = [p + HALF_STEP * c for p, c in zip(perm, cond, strict=True)]
    source = [TIMESTEP / d for d in denominator]
    update = [(p - HALF_STEP * c) / d for p, c, d in zip(perm, cond, denominator, strict=True)]
    return widen(source, width), widen(update, width)


def edge_kernel(e, m, ae, am, labels, perms, conds, near, far, perm, cond, e_last, m_last, ae_last, am_last, e_first, ae_first, marks, sems):
    _, _, depth, rows, width = e.shape
    last = rows - 1
    planes = pl.ds(0, depth)
    moves = (
        (perms, perm),
        (conds, cond),
        (ae.at[0, :, :, last], ae_last.at[:, planes]),
        (ae.at[0, pl.ds(1, 2), :, 0], ae_first.at[:, planes]),
        (labels.at[:, last], marks.at[0, planes]),
        (labels.at[:, 0], marks.at[1, planes]),
        (e.at[0, :, :, last], e_last.at[:, planes]),
        (e.at[0, pl.ds(1, 2), :, 0], e_first.at[:, planes]),
        (m.at[0, pl.ds(1, 2), :, last], m_last.at[:, planes]),
        (am.at[0, pl.ds(1, 2), :, last], am_last.at[:, planes]),
    )
    copies = [pltpu.make_async_copy(src, dst, sems.at[i]) for i, (src, dst) in enumerate(moves)]
    for copy in copies:
        copy.start()
    odd = lax.rem(lax.axis_index("tile"), 2) == 1

    def plane_next(value):
        return jnp.where(row_iota(value.shape) < depth - 1, pltpu.roll(value, EDGE - 1, 0), 0.0)

    for copy in copies:
        copy.wait()
    source, _ = gains(perm, cond, width)
    last_gain, first_gain = (look_up(marks[i], source) for i in range(2))
    ex, ey, ez = (e_last[c] for c in range(3))
    sx, sy, sz = (last_gain * ae_last[c] for c in range(3))
    up = (
        m_last[0] - TIMESTEP * ((plane_next(ex) - ex) + ez),
        m_last[1] + TIMESTEP * (ey + (lane_next(ex) - ex)),
        am_last[0] + ((plane_next(sx) - sx) + sz),
        am_last[1] - (sy + (lane_next(sx) - sx)),
    )
    down = (e_first[0], e_first[1], first_gain * ae_first[0], first_gain * ae_first[1])
    for i, (above, below) in enumerate(zip(up, down, strict=True)):
        at = i * depth
        near[at : at + depth, :] = jnp.where(odd, below, above)[:depth]
        far[at : at + depth, :] = jnp.where(odd, above, below)[:depth]


def from_tiles(near, far):
    odd = lax.rem(lax.axis_index("tile"), 2) == 1

    def above(i):
        return jnp.where(odd, near[i : i + 1, :], far[i : i + 1, :])

    def below(i):
        return jnp.where(odd, far[i : i + 1, :], near[i : i + 1, :])

    return above, below


def pack(planes, share, ports):
    rows = planes[0].shape[0]
    lane = lane_iota((rows, LANES))
    blocks = []
    for port in range(ports):
        tile, offset = divmod(port * share, LANES)
        pieces = []
        for j, plane in enumerate(planes):
            piece = plane[:, tile * LANES : (tile + 1) * LANES]
            if offset + share > LANES:
                piece = jnp.where(
                    lane >= offset, piece, plane[:, (tile + 1) * LANES : (tile + 2) * LANES]
                )
            shift = (j * share - offset) % LANES
            pieces.append(pltpu.roll(piece, shift, 1) if shift else piece)
        block = pieces[-1]
        for j in range(len(planes) - 2, -1, -1):
            block = jnp.where(lane < (j + 1) * share, pieces[j], block)
        blocks.append(block)
    return blocks


def correlation_kernel(ports, e, m, ae, near, far, cells, amplitude, packed, stage, sems):
    _, _, depth, rows, width = e.shape
    share = width // ports
    tile = lax.axis_index("tile")
    above, below = from_tiles(near, far)
    plane_cells = lax.axis_size("tile") * rows * width
    target = cells[0] - tile * (rows * width)
    inside = jnp.where(tile > 0, 1.0, 0.0)
    position = row_iota((rows, width)) * width + lane_iota((rows, width))

    def at(ref, c, z):
        return ref[0, c, z] if z < depth else jnp.zeros((rows, width), jnp.float32)

    zero = jnp.zeros((rows, width), jnp.float32)
    fx_prev, fy_prev = zero, zero
    sums_a, sums_b, copies = [], [], []
    for z in range(depth):
        ex, ey, ez = (at(e, c, z) for c in range(3))
        next_y, next_z = below(z), below(depth + z)
        fx = at(m, 0, z) - TIMESTEP * ((lane_next(ez) - ez) - (at(e, 1, z + 1) - ey))
        fy = at(m, 1, z) - TIMESTEP * ((at(e, 0, z + 1) - ex) - (row_next(ez, next_z) - ez))
        fz = at(m, 2, z) - TIMESTEP * ((row_next(ey, next_y) - ey) - (lane_next(ex) - ex))
        prev_y = inside * (above(z) + TIMESTEP * ez[0:1])
        prev_z = inside * (above(depth + z) - TIMESTEP * ey[0:1])
        hit = position == target - z * plane_cells
        drive_x = ((fz - lane_prev(fz)) - (fy - fy_prev)) - jnp.where(hit, amplitude[0, 0], 0.0)
        drive_y = ((fx - fx_prev) - (fz - row_prev(fz, prev_z))) - jnp.where(hit, amplitude[0, 1], 0.0)
        drive_z = ((fy - row_prev(fy, prev_y)) - (fx - lane_prev(fx))) - jnp.where(
            hit, amplitude[0, 2], 0.0
        )
        ax, ay, az = (at(ae, c, z) for c in range(3))
        sums_a.append(ax * ex + ay * ey + az * ez)
        sums_b.append(ax * drive_x + ay * drive_y + az * drive_z)
        fx_prev, fy_prev = fx, fy
        if z % PLANES == PLANES - 1:
            group = z // PLANES
            for f, sums in enumerate((sums_a, sums_b)):
                slab = f * (depth // PLANES) + group
                for port, block in enumerate(pack(sums, share, ports)):
                    stage[port, slab] = block
                copies.append(pltpu.make_async_copy(stage.at[:, slab], packed.at[:, slab], sems.at[slab]))
                copies[-1].start()
            sums_a, sums_b = [], []
    for copy in copies:
        copy.wait()


def share_factors(ports, labels, perm, cond, factors):
    depth, rows, width = labels.shape
    share = width // ports
    begin = lax.axis_index("port") * share
    perms, conds = region_values(perm, cond)
    denominators = [p + HALF_STEP * c for p, c in zip(perms, conds, strict=True)]
    scales = [TIMESTEP / (d * d) for d in denominators]
    lane = lane_iota((rows, LANES))
    for group in range(depth // PLANES):
        mine = None
        for j in range(PLANES - 1, -1, -1):
            shift = lax.rem(width - begin + j * share, width)
            piece = pltpu.roll(labels[group * PLANES + j], shift, 1)[:, :LANES]
            mine = piece if mine is None else jnp.where(lane < (j + 1) * share, piece, mine)
        for i, entries in enumerate((scales, perms, conds)):
            factors[i, group] = look_up(mine, entries)


def field_kernel(ports, ae, am, labels, near, far, perm, cond, new_e, new_m, factors):
    depth, rows, width = labels.shape
    share_factors(ports, labels, perm, cond, factors)
    source, update = gains(perm, cond, width)
    above, below = from_tiles(near, far)
    inside = jnp.where(lax.axis_index("tile") > 0, 1.0, 0.0)
    zero = jnp.zeros((rows, width), jnp.float32)

    def scaled(z):
        if z == depth:
            return [zero] * 3
        gain = look_up(labels[z], source)
        return [gain * ae[0, c, z] for c in range(3)]

    nx_prev, ny_prev = zero, zero
    here = scaled(0)
    for z in range(depth):
        after = scaled(z + 1)
        sx, sy, sz = here
        next_y = below(2 * depth + z)
        next_z = below(3 * depth + z)
        nx = am[0, 0, z] + ((lane_next(sz) - sz) - (after[1] - sy))
        ny = am[0, 1, z] + ((after[0] - sx) - (row_next(sz, next_z) - sz))
        nz = am[0, 2, z] + ((row_next(sy, next_y) - sy) - (lane_next(sx) - sx))
        prev_y = inside * (above(2 * depth + z) - sz[0:1])
        prev_z = inside * (above(3 * depth + z) + sy[0:1])
        new_m[0, 0, z] = nx
        new_m[0, 1, z] = ny
        new_m[0, 2, z] = nz
        gain = look_up(labels[z], update)
        new_e[0, 0, z] = gain * ae[0, 0, z] - TIMESTEP * ((nz - lane_prev(nz)) - (ny - ny_prev))
        new_e[0, 1, z] = gain * ae[0, 1, z] - TIMESTEP * ((nx - nx_prev) - (nz - row_prev(nz, prev_z)))
        new_e[0, 2, z] = gain * ae[0, 2, z] - TIMESTEP * ((ny - row_prev(ny, prev_y)) - (nx - lane_prev(nx)))
        nx_prev, ny_prev = nx, ny
        here = after


def gradient_kernel(gathered, factors, grad_perm, grad_cond):
    ports, slabs, rows, _ = gathered.shape
    depth, _, share = grad_perm.shape
    groups = depth // PLANES
    sums = []
    for slab in range(slabs):
        total = gathered[0, slab]
        for port in range(1, ports):
            total = total + gathered[port, slab]
        sums.append(total)
    for group in range(groups):
        corr_a, corr_b = sums[group], sums[groups + group]
        factor, permittivity, conductivity = (factors[i, group] for i in range(3))
        by_perm = factor * (conductivity * corr_a - corr_b)
        by_cond = factor * (-permittivity * corr_a - HALF_STEP * corr_b)
        for j in range(PLANES):
            for ref, value in ((grad_perm, by_perm), (grad_cond, by_cond)):
                moved = pltpu.roll(value, LANES - j * share, 1) if j else value
                ref[group * PLANES + j] = moved[:, :share]


def call(kernel, inputs, spaces, outs, out_spaces, flops, moved, scratch=()):
    inputs = [pltpu.with_memory_space_constraint(x, space) if space in (VMEM, HBM) else x for x, space in zip(inputs, spaces, strict=True)]
    return pl.pallas_call(
        kernel,
        out_shape=tuple(space(out.shape, out.dtype) if space is VMEM else out for out, space in zip(outs, out_spaces, strict=True)),
        in_specs=[pl.BlockSpec(memory_space=VMEM if space is HBM_BLOCK else space) for space in spaces],
        out_specs=tuple(pl.BlockSpec(memory_space=VMEM if space is HBM_BLOCK else space) for space in out_spaces),
        scratch_shapes=scratch,
        compiler_params=pltpu.CompilerParams(vmem_limit_bytes=VMEM_LIMIT),
        cost_estimate=pl.CostEstimate(flops=flops, bytes_accessed=moved, transcendentals=0),
    )(*inputs)


def on_device(
    electric,
    magnetic,
    adjoint_electric,
    adjoint_magnetic,
    region_labels,
    permittivity_table,
    conductivity_table,
    port_cells,
    port_amplitude,
):
    depth, rows, width = region_labels.shape
    ports = lax.axis_size("port")
    share = width // ports
    cells = depth * rows * width

    def array(*shape):
        return jax.ShapeDtypeStruct(shape, jnp.float32)

    edge = array(4 * depth, width)
    near, far = call(
        edge_kernel,
        (electric, magnetic, adjoint_electric, adjoint_magnetic, region_labels, permittivity_table, conductivity_table),
        (HBM,) * 7,
        (edge, edge),
        (VMEM, VMEM),
        10 * cells,
        cells * 4 * 14,
        [SMEM(permittivity_table.shape, jnp.float32)] * 2 + [
            VMEM((count, EDGE, width), jnp.float32) for count in (3, 2, 3, 2, 2, 2)
        ] + [VMEM((2, EDGE, width), jnp.int32), pltpu.SemaphoreType.DMA((10,))],
    )
    near, far = swap(near, "tile", 0), swap(far, "tile", 1)
    shares = array(ports, 2 * depth // PLANES, rows, LANES)
    (packed,) = call(
        functools.partial(correlation_kernel, ports),
        (electric, magnetic, adjoint_electric, near, far, port_cells, port_amplitude),
        (VMEM,) * 5 + (SMEM,) * 2,
        (shares,),
        (HBM,),
        60 * cells,
        cells * 4 * 11,
        [VMEM(shares.shape, jnp.float32), pltpu.SemaphoreType.DMA((shares.shape[1],))],
    )
    gathered = lax.all_to_all(packed, "port", 0, 0, tiled=True)
    new_electric, new_magnetic, factors = call(
        functools.partial(field_kernel, ports),
        (adjoint_electric, adjoint_magnetic, region_labels, near, far, permittivity_table, conductivity_table),
        (VMEM, HBM_BLOCK, HBM_BLOCK, VMEM, VMEM) + (SMEM,) * 2,
        (array(1, 3, depth, rows, width), array(1, 3, depth, rows, width), array(3, depth // PLANES, rows, LANES)),
        (HBM_BLOCK, HBM_BLOCK, VMEM),
        80 * cells,
        cells * 4 * 13,
    )
    gradient = array(depth, rows, share)
    gradient_perm, gradient_cond = call(
        gradient_kernel,
        (gathered, factors),
        (VMEM,) * 2,
        (gradient, gradient),
        (HBM_BLOCK,) * 2,
        4 * cells,
        cells * 4 * 3,
    )
    return (new_electric, new_magnetic, gradient_perm, gradient_cond)


def solution(mesh):
    return jax.shard_map(
        on_device,
        mesh=mesh,
        in_specs=(
            P("port", None, None, "tile", None),
            P("port", None, None, "tile", None),
            P("port", None, None, "tile", None),
            P("port", None, None, "tile", None),
            P(None, "tile", None),
            P(),
            P(),
            P("port"),
            P("port", None),
        ),
        out_specs=(
            P("port", None, None, "tile", None),
            P("port", None, None, "tile", None),
            P(None, "tile", "port"),
            P(None, "tile", "port"),
        ),
        check_vma=False,
    )
```

```python
import functools

import jax
import jax.numpy as jnp
from jax import lax
from jax.experimental import pallas as pl
from jax.experimental.pallas import tpu as pltpu
from jax.sharding import PartitionSpec as P

TIMESTEP = 0.5
HALF_STEP = 0.25
PLANES = 3
LANES = 128
EDGE = 8
VMEM_LIMIT = 12 << 20
VMEM = pltpu.VMEM
SMEM = pltpu.SMEM
HBM = pltpu.HBM
HBM_BLOCK = None


def swap(value, axis, first):
    pairs = range(first, lax.axis_size(axis) - 1, 2)
    return lax.ppermute(value, axis, [(i, i + 1) for i in pairs] + [(i + 1, i) for i in pairs])


def lane_iota(shape):
    return lax.broadcasted_iota(jnp.int32, shape, len(shape) - 1)


def row_iota(shape):
    return lax.broadcasted_iota(jnp.int32, shape, len(shape) - 2)


def lane_next(value):
    width = value.shape[1]
    return jnp.where(lane_iota(value.shape) == width - 1, 0.0, pltpu.roll(value, width - 1, 1))


def lane_prev(value):
    return jnp.where(lane_iota(value.shape) == 0, 0.0, pltpu.roll(value, 1, 1))


def row_next(value, beyond):
    rows = value.shape[0]
    return jnp.where(row_iota(value.shape) == rows - 1, beyond, pltpu.roll(value, rows - 1, 0))


def row_prev(value, before):
    return jnp.where(row_iota(value.shape) == 0, before, pltpu.roll(value, 1, 0))


def look_up(labels, entries):
    count = len(entries)
    level = list(entries)
    bit = 1
    while len(level) > 1:
        odd = (labels & bit) != 0
        level = [
            jnp.where(odd, level[i + 1], level[i]) if i + 1 < len(level) else level[i]
            for i in range(0, len(level), 2)
        ]
        bit *= 2
    assert count <= bit
    return level[0]


def region_values(perm_ref, cond_ref):
    shape = (1, LANES)
    perm = [jnp.full(shape, perm_ref[r], jnp.float32) for r in range(perm_ref.shape[0])]
    cond = [jnp.full(shape, cond_ref[r], jnp.float32) for r in range(cond_ref.shape[0])]
    return perm, cond


def widen(entries, width):
    return [jnp.concatenate([entry] * (width // LANES), axis=1) for entry in entries]


def gains(perm_ref, cond_ref, width):
    perm, cond = region_values(perm_ref, cond_ref)
    denominator = [p + HALF_STEP * c for p, c in zip(perm, cond, strict=True)]
    source = [TIMESTEP / d for d in denominator]
    update = [(p - HALF_STEP * c) / d for p, c, d in zip(perm, cond, denominator, strict=True)]
    return widen(source, width), widen(update, width)


def edge_kernel(e, m, ae, am, labels, perms, conds, far, near, perm, cond, e_last, m_last, ae_last, am_last, e_first, ae_first, marks, sems):
    _, _, depth, rows, width = e.shape
    last = rows - 1
    planes = pl.ds(0, depth)
    moves = (
        (perms, perm),
        (conds, cond),
        (ae.at[0, :, :, last], ae_last.at[:, planes]),
        (ae.at[0, pl.ds(1, 2), :, 0], ae_first.at[:, planes]),
        (labels.at[:, last], marks.at[0, planes]),
        (labels.at[:, 0], marks.at[1, planes]),
        (e.at[0, :, :, last], e_last.at[:, planes]),
        (e.at[0, pl.ds(1, 2), :, 0], e_first.at[:, planes]),
        (m.at[0, pl.ds(1, 2), :, last], m_last.at[:, planes]),
        (am.at[0, pl.ds(1, 2), :, last], am_last.at[:, planes]),
    )
    copies = [pltpu.make_async_copy(src, dst, sems.at[i]) for i, (src, dst) in enumerate(moves)]
    for copy in copies:
        copy.start()
    odd = lax.rem(lax.axis_index("tile"), 2) == 1

    def plane_next(value):
        return jnp.where(row_iota(value.shape) < depth - 1, pltpu.roll(value, EDGE - 1, 0), 0.0)

    for copy in copies:
        copy.wait()
    source, _ = gains(perm, cond, width)
    last_gain, first_gain = (look_up(marks[i], source) for i in range(2))
    ex, ey, ez = (e_last[c] for c in range(3))
    sx, sy, sz = (last_gain * ae_last[c] for c in range(3))
    up = (
        m_last[0] - TIMESTEP * ((plane_next(ex) - ex) + ez),
        m_last[1] + TIMESTEP * (ey + (lane_next(ex) - ex)),
        am_last[0] + ((plane_next(sx) - sx) + sz),
        am_last[1] - (sy + (lane_next(sx) - sx)),
    )
    down = (e_first[0], e_first[1], first_gain * ae_first[0], first_gain * ae_first[1])
    for i, (above, below) in enumerate(zip(up, down, strict=True)):
        at = i * depth
        near[at : at + depth, :] = jnp.where(odd, below, above)[:depth]
        far[at : at + depth, :] = jnp.where(odd, above, below)[:depth]


def from_tiles(near, far):
    odd = lax.rem(lax.axis_index("tile"), 2) == 1

    def above(i):
        return jnp.where(odd, near[i : i + 1, :], far[i : i + 1, :])

    def below(i):
        return jnp.where(odd, far[i : i + 1, :], near[i : i + 1, :])

    return above, below


def pack(planes, share, ports):
    rows = planes[0].shape[0]
    lane = lane_iota((rows, LANES))
    blocks = []
    for port in range(ports):
        tile, offset = divmod(port * share, LANES)
        pieces = []
        for j, plane in enumerate(planes):
            piece = plane[:, tile * LANES : (tile + 1) * LANES]
            if offset + share > LANES:
                piece = jnp.where(
                    lane >= offset, piece, plane[:, (tile + 1) * LANES : (tile + 2) * LANES]
                )
            shift = (j * share - offset) % LANES
            pieces.append(pltpu.roll(piece, shift, 1) if shift else piece)
        block = pieces[-1]
        for j in range(len(planes) - 2, -1, -1):
            block = jnp.where(lane < (j + 1) * share, pieces[j], block)
        blocks.append(block)
    return blocks


def correlation_kernel(ports, e, m, ae, far, near, cells, amplitude, packed, stage, sems):
    _, _, depth, rows, width = e.shape
    share = width // ports
    tile = lax.axis_index("tile")
    above, below = from_tiles(near, far)
    plane_cells = lax.axis_size("tile") * rows * width
    target = cells[0] - tile * (rows * width)
    inside = jnp.where(tile > 0, 1.0, 0.0)
    position = row_iota((rows, width)) * width + lane_iota((rows, width))

    def at(ref, c, z):
        return ref[0, c, z] if z < depth else jnp.zeros((rows, width), jnp.float32)

    zero = jnp.zeros((rows, width), jnp.float32)
    fx_prev, fy_prev = zero, zero
    sums_a, sums_b, copies = [], [], []
    for z in range(depth):
        ex, ey, ez = (at(e, c, z) for c in range(3))
        next_y, next_z = below(z), below(depth + z)
        fx = at(m, 0, z) - TIMESTEP * ((lane_next(ez) - ez) - (at(e, 1, z + 1) - ey))
        fy = at(m, 1, z) - TIMESTEP * ((at(e, 0, z + 1) - ex) - (row_next(ez, next_z) - ez))
        fz = at(m, 2, z) - TIMESTEP * ((row_next(ey, next_y) - ey) - (lane_next(ex) - ex))
        prev_y = inside * (above(z) + TIMESTEP * ez[0:1])
        prev_z = inside * (above(depth + z) - TIMESTEP * ey[0:1])
        hit = position == target - z * plane_cells
        drive_x = ((fz - lane_prev(fz)) - (fy - fy_prev)) - jnp.where(hit, amplitude[0, 0], 0.0)
        drive_y = ((fx - fx_prev) - (fz - row_prev(fz, prev_z))) - jnp.where(hit, amplitude[0, 1], 0.0)
        drive_z = ((fy - row_prev(fy, prev_y)) - (fx - lane_prev(fx))) - jnp.where(
            hit, amplitude[0, 2], 0.0
        )
        ax, ay, az = (at(ae, c, z) for c in range(3))
        sums_a.append(ax * ex + ay * ey + az * ez)
        sums_b.append(ax * drive_x + ay * drive_y + az * drive_z)
        fx_prev, fy_prev = fx, fy
        if z % PLANES == PLANES - 1:
            group = z // PLANES
            for f, sums in enumerate((sums_a, sums_b)):
                slab = f * (depth // PLANES) + group
                for port, block in enumerate(pack(sums, share, ports)):
                    stage[port, slab] = block
                copies.append(pltpu.make_async_copy(stage.at[:, slab], packed.at[:, slab], sems.at[slab]))
                copies[-1].start()
            sums_a, sums_b = [], []
    for copy in copies:
        copy.wait()


def share_factors(ports, labels, perm, cond, factors):
    depth, rows, width = labels.shape
    share = width // ports
    begin = lax.axis_index("port") * share
    perms, conds = region_values(perm, cond)
    denominators = [p + HALF_STEP * c for p, c in zip(perms, conds, strict=True)]
    scales = [TIMESTEP / (d * d) for d in denominators]
    lane = lane_iota((rows, LANES))
    for group in range(depth // PLANES):
        mine = None
        for j in range(PLANES - 1, -1, -1):
            shift = lax.rem(width - begin + j * share, width)
            piece = pltpu.roll(labels[group * PLANES + j], shift, 1)[:, :LANES]
            mine = piece if mine is None else jnp.where(lane < (j + 1) * share, piece, mine)
        for i, entries in enumerate((scales, perms, conds)):
            factors[i, group] = look_up(mine, entries)


def field_kernel(ports, ae, am, labels, far, near, perm, cond, new_e, new_m, factors):
    depth, rows, width = labels.shape
    share_factors(ports, labels, perm, cond, factors)
    source, update = gains(perm, cond, width)
    above, below = from_tiles(near, far)
    inside = jnp.where(lax.axis_index("tile") > 0, 1.0, 0.0)
    zero = jnp.zeros((rows, width), jnp.float32)

    def scaled(z):
        if z == depth:
            return [zero] * 3
        gain = look_up(labels[z], source)
        return [gain * ae[0, c, z] for c in range(3)]

    nx_prev, ny_prev = zero, zero
    here = scaled(0)
    for z in range(depth):
        after = scaled(z + 1)
        sx, sy, sz = here
        next_y = below(2 * depth + z)
        next_z = below(3 * depth + z)
        nx = am[0, 0, z] + ((lane_next(sz) - sz) - (after[1] - sy))
        ny = am[0, 1, z] + ((after[0] - sx) - (row_next(sz, next_z) - sz))
        nz = am[0, 2, z] + ((row_next(sy, next_y) - sy) - (lane_next(sx) - sx))
        prev_y = inside * (above(2 * depth + z) - sz[0:1])
        prev_z = inside * (above(3 * depth + z) + sy[0:1])
        new_m[0, 0, z] = nx
        new_m[0, 1, z] = ny
        new_m[0, 2, z] = nz
        gain = look_up(labels[z], update)
        new_e[0, 0, z] = gain * ae[0, 0, z] - TIMESTEP * ((nz - lane_prev(nz)) - (ny - ny_prev))
        new_e[0, 1, z] = gain * ae[0, 1, z] - TIMESTEP * ((nx - nx_prev) - (nz - row_prev(nz, prev_z)))
        new_e[0, 2, z] = gain * ae[0, 2, z] - TIMESTEP * ((ny - row_prev(ny, prev_y)) - (nx - lane_prev(nx)))
        nx_prev, ny_prev = nx, ny
        here = after


def gradient_kernel(gathered, factors, grad_perm, grad_cond):
    ports, slabs, rows, _ = gathered.shape
    depth, _, share = grad_perm.shape
    groups = depth // PLANES
    sums = []
    for slab in range(slabs):
        total = gathered[0, slab]
        for port in range(1, ports):
            total = total + gathered[port, slab]
        sums.append(total)
    for group in range(groups):
        corr_a, corr_b = sums[group], sums[groups + group]
        factor, permittivity, conductivity = (factors[i, group] for i in range(3))
        by_perm = factor * (conductivity * corr_a - corr_b)
        by_cond = factor * (-permittivity * corr_a - HALF_STEP * corr_b)
        for j in range(PLANES):
            for ref, value in ((grad_perm, by_perm), (grad_cond, by_cond)):
                moved = pltpu.roll(value, LANES - j * share, 1) if j else value
                ref[group * PLANES + j] = moved[:, :share]


def call(kernel, inputs, spaces, outs, out_spaces, flops, moved, scratch=()):
    inputs = [pltpu.with_memory_space_constraint(x, space) if space in (VMEM, HBM) else x for x, space in zip(inputs, spaces, strict=True)]
    return pl.pallas_call(
        kernel,
        out_shape=tuple(space(out.shape, out.dtype) if space is VMEM else out for out, space in zip(outs, out_spaces, strict=True)),
        in_specs=[pl.BlockSpec(memory_space=VMEM if space is HBM_BLOCK else space) for space in spaces],
        out_specs=tuple(pl.BlockSpec(memory_space=VMEM if space is HBM_BLOCK else space) for space in out_spaces),
        scratch_shapes=scratch,
        compiler_params=pltpu.CompilerParams(vmem_limit_bytes=VMEM_LIMIT),
        cost_estimate=pl.CostEstimate(flops=flops, bytes_accessed=moved, transcendentals=0),
    )(*inputs)


def on_device(
    electric,
    magnetic,
    adjoint_electric,
    adjoint_magnetic,
    region_labels,
    permittivity_table,
    conductivity_table,
    port_cells,
    port_amplitude,
):
    depth, rows, width = region_labels.shape
    ports = lax.axis_size("port")
    share = width // ports
    cells = depth * rows * width

    def array(*shape):
        return jax.ShapeDtypeStruct(shape, jnp.float32)

    edge = array(4 * depth, width)
    far, near = call(
        edge_kernel,
        (electric, magnetic, adjoint_electric, adjoint_magnetic, region_labels, permittivity_table, conductivity_table),
        (HBM,) * 7,
        (edge, edge),
        (VMEM, VMEM),
        10 * cells,
        cells * 4 * 14,
        [SMEM(permittivity_table.shape, jnp.float32)] * 2 + [
            VMEM((count, EDGE, width), jnp.float32) for count in (3, 2, 3, 2, 2, 2)
        ] + [VMEM((2, EDGE, width), jnp.int32), pltpu.SemaphoreType.DMA((10,))],
    )
    far = swap(far, "tile", 1)
    near = swap(near, "tile", 0)
    shares = array(ports, 2 * depth // PLANES, rows, LANES)
    (packed,) = call(
        functools.partial(correlation_kernel, ports),
        (electric, magnetic, adjoint_electric, far, near, port_cells, port_amplitude),
        (VMEM,) * 5 + (SMEM,) * 2,
        (shares,),
        (HBM,),
        60 * cells,
        cells * 4 * 11,
        [VMEM(shares.shape, jnp.float32), pltpu.SemaphoreType.DMA((shares.shape[1],))],
    )
    gathered = lax.all_to_all(packed, "port", 0, 0, tiled=True)
    new_electric, new_magnetic, factors = call(
        functools.partial(field_kernel, ports),
        (adjoint_electric, adjoint_magnetic, region_labels, far, near, permittivity_table, conductivity_table),
        (VMEM, HBM_BLOCK, HBM_BLOCK, VMEM, VMEM) + (SMEM,) * 2,
        (array(1, 3, depth, rows, width), array(1, 3, depth, rows, width), array(3, depth // PLANES, rows, LANES)),
        (HBM_BLOCK, HBM_BLOCK, VMEM),
        80 * cells,
        cells * 4 * 13,
    )
    gradient = array(depth, rows, share)
    gradient_perm, gradient_cond = call(
        gradient_kernel,
        (gathered, factors),
        (VMEM,) * 2,
        (gradient, gradient),
        (HBM_BLOCK,) * 2,
        4 * cells,
        cells * 4 * 3,
    )
    return (new_electric, new_magnetic, gradient_perm, gradient_cond)


def solution(mesh):
    return jax.shard_map(
        on_device,
        mesh=mesh,
        in_specs=(
            P("port", None, None, "tile", None),
            P("port", None, None, "tile", None),
            P("port", None, None, "tile", None),
            P("port", None, None, "tile", None),
            P(None, "tile", None),
            P(),
            P(),
            P("port"),
            P("port", None),
        ),
        out_specs=(
            P("port", None, None, "tile", None),
            P("port", None, None, "tile", None),
            P(None, "tile", "port"),
            P(None, "tile", "port"),
        ),
        check_vma=False,
    )
```

```python
import functools

import jax
import jax.numpy as jnp
from jax import lax
from jax.experimental import pallas as pl
from jax.experimental.pallas import tpu as pltpu
from jax.sharding import PartitionSpec as P

TIMESTEP = 0.5
HALF_STEP = 0.25
PLANES = 3
LANES = 128
EDGE = 8
VMEM_LIMIT = 12 << 20
VMEM = pltpu.VMEM
SMEM = pltpu.SMEM
HBM = pltpu.HBM
HBM_BLOCK = None


def from_behind(value, axis, steps):
    count = lax.axis_size(axis)
    first, last = (max(0, -steps), min(count, count - steps))
    return lax.ppermute(value, axis, [(source, source + steps) for source in range(first, last)])


def lane_iota(shape):
    return lax.broadcasted_iota(jnp.int32, shape, len(shape) - 1)


def row_iota(shape):
    return lax.broadcasted_iota(jnp.int32, shape, len(shape) - 2)


def lane_next(value):
    width = value.shape[1]
    return jnp.where(lane_iota(value.shape) == width - 1, 0.0, pltpu.roll(value, width - 1, 1))


def lane_prev(value):
    return jnp.where(lane_iota(value.shape) == 0, 0.0, pltpu.roll(value, 1, 1))


def row_next(value, beyond):
    rows = value.shape[0]
    return jnp.where(row_iota(value.shape) == rows - 1, beyond, pltpu.roll(value, rows - 1, 0))


def row_prev(value, before):
    return jnp.where(row_iota(value.shape) == 0, before, pltpu.roll(value, 1, 0))


def look_up(labels, entries):
    count = len(entries)
    level = list(entries)
    bit = 1
    while len(level) > 1:
        odd = (labels & bit) != 0
        level = [
            jnp.where(odd, level[i + 1], level[i]) if i + 1 < len(level) else level[i]
            for i in range(0, len(level), 2)
        ]
        bit *= 2
    assert count <= bit
    return level[0]


def region_values(perm_ref, cond_ref):
    shape = (1, LANES)
    perm = [jnp.full(shape, perm_ref[r], jnp.float32) for r in range(perm_ref.shape[0])]
    cond = [jnp.full(shape, cond_ref[r], jnp.float32) for r in range(cond_ref.shape[0])]
    return perm, cond


def widen(entries, width):
    return [jnp.concatenate([entry] * (width // LANES), axis=1) for entry in entries]


def gains(perm_ref, cond_ref, width):
    perm, cond = region_values(perm_ref, cond_ref)
    denominator = [p + HALF_STEP * c for p, c in zip(perm, cond, strict=True)]
    source = [TIMESTEP / d for d in denominator]
    update = [(p - HALF_STEP * c) / d for p, c, d in zip(perm, cond, denominator, strict=True)]
    return widen(source, width), widen(update, width)


def edge_kernel(e, m, ae, am, labels, perms, conds, to_ahead, to_behind, perm, cond, e_last, m_last, ae_last, am_last, e_first, ae_first, marks, sems):
    _, _, depth, rows, width = e.shape
    last = rows - 1
    planes = pl.ds(0, depth)
    moves = (
        (perms, perm),
        (conds, cond),
        (ae.at[0, :, :, last], ae_last.at[:, planes]),
        (ae.at[0, pl.ds(1, 2), :, 0], ae_first.at[:, planes]),
        (labels.at[:, last], marks.at[0, planes]),
        (labels.at[:, 0], marks.at[1, planes]),
        (e.at[0, :, :, last], e_last.at[:, planes]),
        (e.at[0, pl.ds(1, 2), :, 0], e_first.at[:, planes]),
        (m.at[0, pl.ds(1, 2), :, last], m_last.at[:, planes]),
        (am.at[0, pl.ds(1, 2), :, last], am_last.at[:, planes]),
    )
    copies = [pltpu.make_async_copy(src, dst, sems.at[i]) for i, (src, dst) in enumerate(moves)]
    for copy in copies:
        copy.start()
    def plane_next(value):
        return jnp.where(row_iota(value.shape) < depth - 1, pltpu.roll(value, EDGE - 1, 0), 0.0)

    for copy in copies:
        copy.wait()
    source, _ = gains(perm, cond, width)
    last_gain, first_gain = (look_up(marks[i], source) for i in range(2))
    ex, ey, ez = (e_last[c] for c in range(3))
    sx, sy, sz = (last_gain * ae_last[c] for c in range(3))
    up = (
        m_last[0] - TIMESTEP * ((plane_next(ex) - ex) + ez),
        m_last[1] + TIMESTEP * (ey + (lane_next(ex) - ex)),
        am_last[0] + ((plane_next(sx) - sx) + sz),
        am_last[1] - (sy + (lane_next(sx) - sx)),
    )
    down = (e_first[0], e_first[1], first_gain * ae_first[0], first_gain * ae_first[1])
    for i, (above, below) in enumerate(zip(up, down, strict=True)):
        at = i * depth
        to_ahead[at : at + depth, :] = above[:depth]
        to_behind[at : at + depth, :] = below[:depth]


def line_of(ref):
    return lambda i: ref[i : i + 1, :]


def pack(planes, share, ports):
    rows = planes[0].shape[0]
    lane = lane_iota((rows, LANES))
    blocks = []
    for port in range(ports):
        tile, offset = divmod(port * share, LANES)
        pieces = []
        for j, plane in enumerate(planes):
            piece = plane[:, tile * LANES : (tile + 1) * LANES]
            if offset + share > LANES:
                piece = jnp.where(
                    lane >= offset, piece, plane[:, (tile + 1) * LANES : (tile + 2) * LANES]
                )
            shift = (j * share - offset) % LANES
            pieces.append(pltpu.roll(piece, shift, 1) if shift else piece)
        block = pieces[-1]
        for j in range(len(planes) - 2, -1, -1):
            block = jnp.where(lane < (j + 1) * share, pieces[j], block)
        blocks.append(block)
    return blocks


def correlation_kernel(ports, e, m, ae, behind, ahead, cells, amplitude, packed, stage, sems):
    _, _, depth, rows, width = e.shape
    share = width // ports
    tile = lax.axis_index("tile")
    above, below = line_of(behind), line_of(ahead)
    plane_cells = lax.axis_size("tile") * rows * width
    target = cells[0] - tile * (rows * width)
    inside = jnp.where(tile > 0, 1.0, 0.0)
    position = row_iota((rows, width)) * width + lane_iota((rows, width))

    def at(ref, c, z):
        return ref[0, c, z] if z < depth else jnp.zeros((rows, width), jnp.float32)

    zero = jnp.zeros((rows, width), jnp.float32)
    fx_prev, fy_prev = zero, zero
    sums_a, sums_b, copies = [], [], []
    for z in range(depth):
        ex, ey, ez = (at(e, c, z) for c in range(3))
        next_y, next_z = below(z), below(depth + z)
        fx = at(m, 0, z) - TIMESTEP * ((lane_next(ez) - ez) - (at(e, 1, z + 1) - ey))
        fy = at(m, 1, z) - TIMESTEP * ((at(e, 0, z + 1) - ex) - (row_next(ez, next_z) - ez))
        fz = at(m, 2, z) - TIMESTEP * ((row_next(ey, next_y) - ey) - (lane_next(ex) - ex))
        prev_y = inside * (above(z) + TIMESTEP * ez[0:1])
        prev_z = inside * (above(depth + z) - TIMESTEP * ey[0:1])
        hit = position == target - z * plane_cells
        drive_x = ((fz - lane_prev(fz)) - (fy - fy_prev)) - jnp.where(hit, amplitude[0, 0], 0.0)
        drive_y = ((fx - fx_prev) - (fz - row_prev(fz, prev_z))) - jnp.where(hit, amplitude[0, 1], 0.0)
        drive_z = ((fy - row_prev(fy, prev_y)) - (fx - lane_prev(fx))) - jnp.where(
            hit, amplitude[0, 2], 0.0
        )
        ax, ay, az = (at(ae, c, z) for c in range(3))
        sums_a.append(ax * ex + ay * ey + az * ez)
        sums_b.append(ax * drive_x + ay * drive_y + az * drive_z)
        fx_prev, fy_prev = fx, fy
        if z % PLANES == PLANES - 1:
            group = z // PLANES
            for f, sums in enumerate((sums_a, sums_b)):
                slab = f * (depth // PLANES) + group
                for port, block in enumerate(pack(sums, share, ports)):
                    stage[port, slab] = block
                copies.append(pltpu.make_async_copy(stage.at[:, slab], packed.at[:, slab], sems.at[slab]))
                copies[-1].start()
            sums_a, sums_b = [], []
    for copy in copies:
        copy.wait()


def share_factors(ports, labels, perm, cond, factors):
    depth, rows, width = labels.shape
    share = width // ports
    begin = lax.axis_index("port") * share
    perms, conds = region_values(perm, cond)
    denominators = [p + HALF_STEP * c for p, c in zip(perms, conds, strict=True)]
    scales = [TIMESTEP / (d * d) for d in denominators]
    lane = lane_iota((rows, LANES))
    for group in range(depth // PLANES):
        mine = None
        for j in range(PLANES - 1, -1, -1):
            shift = lax.rem(width - begin + j * share, width)
            piece = pltpu.roll(labels[group * PLANES + j], shift, 1)[:, :LANES]
            mine = piece if mine is None else jnp.where(lane < (j + 1) * share, piece, mine)
        for i, entries in enumerate((scales, perms, conds)):
            factors[i, group] = look_up(mine, entries)


def field_kernel(ports, ae, am, labels, behind, ahead, perm, cond, new_e, new_m, factors):
    depth, rows, width = labels.shape
    share_factors(ports, labels, perm, cond, factors)
    source, update = gains(perm, cond, width)
    above, below = line_of(behind), line_of(ahead)
    inside = jnp.where(lax.axis_index("tile") > 0, 1.0, 0.0)
    zero = jnp.zeros((rows, width), jnp.float32)

    def scaled(z):
        if z == depth:
            return [zero] * 3
        gain = look_up(labels[z], source)
        return [gain * ae[0, c, z] for c in range(3)]

    nx_prev, ny_prev = zero, zero
    here = scaled(0)
    for z in range(depth):
        after = scaled(z + 1)
        sx, sy, sz = here
        next_y = below(2 * depth + z)
        next_z = below(3 * depth + z)
        nx = am[0, 0, z] + ((lane_next(sz) - sz) - (after[1] - sy))
        ny = am[0, 1, z] + ((after[0] - sx) - (row_next(sz, next_z) - sz))
        nz = am[0, 2, z] + ((row_next(sy, next_y) - sy) - (lane_next(sx) - sx))
        prev_y = inside * (above(2 * depth + z) - sz[0:1])
        prev_z = inside * (above(3 * depth + z) + sy[0:1])
        new_m[0, 0, z] = nx
        new_m[0, 1, z] = ny
        new_m[0, 2, z] = nz
        gain = look_up(labels[z], update)
        new_e[0, 0, z] = gain * ae[0, 0, z] - TIMESTEP * ((nz - lane_prev(nz)) - (ny - ny_prev))
        new_e[0, 1, z] = gain * ae[0, 1, z] - TIMESTEP * ((nx - nx_prev) - (nz - row_prev(nz, prev_z)))
        new_e[0, 2, z] = gain * ae[0, 2, z] - TIMESTEP * ((ny - row_prev(ny, prev_y)) - (nx - lane_prev(nx)))
        nx_prev, ny_prev = nx, ny
        here = after


def gradient_kernel(gathered, factors, grad_perm, grad_cond):
    ports, slabs, rows, _ = gathered.shape
    depth, _, share = grad_perm.shape
    groups = depth // PLANES
    sums = []
    for slab in range(slabs):
        total = gathered[0, slab]
        for port in range(1, ports):
            total = total + gathered[port, slab]
        sums.append(total)
    for group in range(groups):
        corr_a, corr_b = sums[group], sums[groups + group]
        factor, permittivity, conductivity = (factors[i, group] for i in range(3))
        by_perm = factor * (conductivity * corr_a - corr_b)
        by_cond = factor * (-permittivity * corr_a - HALF_STEP * corr_b)
        for j in range(PLANES):
            for ref, value in ((grad_perm, by_perm), (grad_cond, by_cond)):
                moved = pltpu.roll(value, LANES - j * share, 1) if j else value
                ref[group * PLANES + j] = moved[:, :share]


def call(kernel, inputs, spaces, outs, out_spaces, flops, moved, scratch=()):
    inputs = [pltpu.with_memory_space_constraint(x, space) if space in (VMEM, HBM) else x for x, space in zip(inputs, spaces, strict=True)]
    return pl.pallas_call(
        kernel,
        out_shape=tuple(space(out.shape, out.dtype) if space is VMEM else out for out, space in zip(outs, out_spaces, strict=True)),
        in_specs=[pl.BlockSpec(memory_space=VMEM if space is HBM_BLOCK else space) for space in spaces],
        out_specs=tuple(pl.BlockSpec(memory_space=VMEM if space is HBM_BLOCK else space) for space in out_spaces),
        scratch_shapes=scratch,
        compiler_params=pltpu.CompilerParams(vmem_limit_bytes=VMEM_LIMIT),
        cost_estimate=pl.CostEstimate(flops=flops, bytes_accessed=moved, transcendentals=0),
    )(*inputs)


def on_device(
    electric,
    magnetic,
    adjoint_electric,
    adjoint_magnetic,
    region_labels,
    permittivity_table,
    conductivity_table,
    port_cells,
    port_amplitude,
):
    depth, rows, width = region_labels.shape
    ports = lax.axis_size("port")
    share = width // ports
    cells = depth * rows * width

    def array(*shape):
        return jax.ShapeDtypeStruct(shape, jnp.float32)

    edge = array(4 * depth, width)
    to_ahead, to_behind = call(
        edge_kernel,
        (electric, magnetic, adjoint_electric, adjoint_magnetic, region_labels, permittivity_table, conductivity_table),
        (HBM,) * 7,
        (edge, edge),
        (VMEM, VMEM),
        10 * cells,
        cells * 4 * 14,
        [SMEM(permittivity_table.shape, jnp.float32)] * 2 + [
            VMEM((count, EDGE, width), jnp.float32) for count in (3, 2, 3, 2, 2, 2)
        ] + [VMEM((2, EDGE, width), jnp.int32), pltpu.SemaphoreType.DMA((10,))],
    )
    behind = from_behind(to_ahead, "tile", 1)
    ahead = from_behind(to_behind, "tile", -1)
    shares = array(ports, 2 * depth // PLANES, rows, LANES)
    (packed,) = call(
        functools.partial(correlation_kernel, ports),
        (electric, magnetic, adjoint_electric, behind, ahead, port_cells, port_amplitude),
        (VMEM,) * 5 + (SMEM,) * 2,
        (shares,),
        (HBM,),
        60 * cells,
        cells * 4 * 11,
        [VMEM(shares.shape, jnp.float32), pltpu.SemaphoreType.DMA((shares.shape[1],))],
    )
    gathered = lax.all_to_all(packed, "port", 0, 0, tiled=True)
    new_electric, new_magnetic, factors = call(
        functools.partial(field_kernel, ports),
        (adjoint_electric, adjoint_magnetic, region_labels, behind, ahead, permittivity_table, conductivity_table),
        (VMEM, HBM_BLOCK, HBM_BLOCK, VMEM, VMEM) + (SMEM,) * 2,
        (array(1, 3, depth, rows, width), array(1, 3, depth, rows, width), array(3, depth // PLANES, rows, LANES)),
        (HBM_BLOCK, HBM_BLOCK, VMEM),
        80 * cells,
        cells * 4 * 13,
    )
    gradient = array(depth, rows, share)
    gradient_perm, gradient_cond = call(
        gradient_kernel,
        (gathered, factors),
        (VMEM,) * 2,
        (gradient, gradient),
        (HBM_BLOCK,) * 2,
        4 * cells,
        cells * 4 * 3,
    )
    return (new_electric, new_magnetic, gradient_perm, gradient_cond)


def solution(mesh):
    return jax.shard_map(
        on_device,
        mesh=mesh,
        in_specs=(
            P("port", None, None, "tile", None),
            P("port", None, None, "tile", None),
            P("port", None, None, "tile", None),
            P("port", None, None, "tile", None),
            P(None, "tile", None),
            P(),
            P(),
            P("port"),
            P("port", None),
        ),
        out_specs=(
            P("port", None, None, "tile", None),
            P("port", None, None, "tile", None),
            P(None, "tile", "port"),
            P(None, "tile", "port"),
        ),
        check_vma=False,
    )
```

```python
import functools

import jax
import jax.numpy as jnp
from jax import lax
from jax.experimental import pallas as pl
from jax.experimental.pallas import tpu as pltpu
from jax.sharding import PartitionSpec as P

TIMESTEP = 0.5
HALF_STEP = 0.25
PLANES = 3
LANES = 128
EDGE = 8
VMEM_LIMIT = 12 << 20
VMEM = pltpu.VMEM
SMEM = pltpu.SMEM
HBM = pltpu.HBM
HBM_BLOCK = None


def from_behind(value, axis, steps):
    count = lax.axis_size(axis)
    first, last = (max(0, -steps), min(count, count - steps))
    return lax.ppermute(value, axis, [(source, source + steps) for source in range(first, last)])


def lane_iota(shape):
    return lax.broadcasted_iota(jnp.int32, shape, len(shape) - 1)


def row_iota(shape):
    return lax.broadcasted_iota(jnp.int32, shape, len(shape) - 2)


def lane_next(value):
    width = value.shape[1]
    return jnp.where(lane_iota(value.shape) == width - 1, 0.0, pltpu.roll(value, width - 1, 1))


def lane_prev(value):
    return jnp.where(lane_iota(value.shape) == 0, 0.0, pltpu.roll(value, 1, 1))


def row_next(value, beyond):
    rows = value.shape[0]
    return jnp.where(row_iota(value.shape) == rows - 1, beyond, pltpu.roll(value, rows - 1, 0))


def row_prev(value, before):
    return jnp.where(row_iota(value.shape) == 0, before, pltpu.roll(value, 1, 0))


def look_up(labels, entries):
    count = len(entries)
    level = list(entries)
    bit = 1
    while len(level) > 1:
        odd = (labels & bit) != 0
        level = [
            jnp.where(odd, level[i + 1], level[i]) if i + 1 < len(level) else level[i]
            for i in range(0, len(level), 2)
        ]
        bit *= 2
    assert count <= bit
    return level[0]


def region_values(perm_ref, cond_ref):
    shape = (1, LANES)
    perm = [jnp.full(shape, perm_ref[r], jnp.float32) for r in range(perm_ref.shape[0])]
    cond = [jnp.full(shape, cond_ref[r], jnp.float32) for r in range(cond_ref.shape[0])]
    return perm, cond


def widen(entries, width):
    return [jnp.concatenate([entry] * (width // LANES), axis=1) for entry in entries]


def gains(perm_ref, cond_ref, width):
    perm, cond = region_values(perm_ref, cond_ref)
    denominator = [p + HALF_STEP * c for p, c in zip(perm, cond, strict=True)]
    source = [TIMESTEP / d for d in denominator]
    update = [(p - HALF_STEP * c) / d for p, c, d in zip(perm, cond, denominator, strict=True)]
    return widen(source, width), widen(update, width)


def edge_kernel(e, m, ae, am, labels, perms, conds, to_ahead, to_behind, ae_last, ae_first, e_first, perm, cond, e_last, m_last, am_last, marks, sems):
    _, _, depth, rows, width = e.shape
    last = rows - 1
    planes = pl.ds(0, depth)
    for ref in (ae_last, ae_first, e_first, e_last, m_last, am_last):
        ref[:, depth:, :] = jnp.zeros((ref.shape[0], EDGE - depth, width), jnp.float32)
    moves = (
        (perms, perm),
        (conds, cond),
        (ae.at[0, :, :, last], ae_last.at[:, planes]),
        (ae.at[0, pl.ds(1, 2), :, 0], ae_first.at[:, planes]),
        (labels.at[:, last], marks.at[0, planes]),
        (labels.at[:, 0], marks.at[1, planes]),
        (e.at[0, :, :, last], e_last.at[:, planes]),
        (e.at[0, pl.ds(1, 2), :, 0], e_first.at[:, planes]),
        (m.at[0, pl.ds(1, 2), :, last], m_last.at[:, planes]),
        (am.at[0, pl.ds(1, 2), :, last], am_last.at[:, planes]),
    )
    copies = [pltpu.make_async_copy(src, dst, sems.at[i]) for i, (src, dst) in enumerate(moves)]
    for copy in copies:
        copy.start()
    def plane_next(value):
        return pltpu.roll(value, EDGE - 1, 0)

    for copy in copies:
        copy.wait()
    source, _ = gains(perm, cond, width)
    last_gain, first_gain = (look_up(marks[i], source) for i in range(2))
    ex, ey, ez = (e_last[c] for c in range(3))
    sx, sy, sz = (last_gain * ae_last[c] for c in range(3))
    up = (
        m_last[0] - TIMESTEP * ((plane_next(ex) - ex) + ez),
        m_last[1] + TIMESTEP * (ey + (lane_next(ex) - ex)),
        am_last[0] + ((plane_next(sx) - sx) + sz),
        am_last[1] - (sy + (lane_next(sx) - sx)),
    )
    down = (e_first[0], e_first[1], first_gain * ae_first[0], first_gain * ae_first[1])
    for i, (above, below) in enumerate(zip(up, down, strict=True)):
        at = i * depth
        to_ahead[at : at + depth, :] = above[:depth]
        to_behind[at : at + depth, :] = below[:depth]


def line_of(ref):
    return lambda i: ref[i : i + 1, :]


def pack(planes, share, ports):
    rows = planes[0].shape[0]
    lane = lane_iota((rows, LANES))
    blocks = []
    for port in range(ports):
        tile, offset = divmod(port * share, LANES)
        pieces = []
        for j, plane in enumerate(planes):
            piece = plane[:, tile * LANES : (tile + 1) * LANES]
            if offset + share > LANES:
                piece = jnp.where(
                    lane >= offset, piece, plane[:, (tile + 1) * LANES : (tile + 2) * LANES]
                )
            shift = (j * share - offset) % LANES
            pieces.append(pltpu.roll(piece, shift, 1) if shift else piece)
        block = pieces[-1]
        for j in range(len(planes) - 2, -1, -1):
            block = jnp.where(lane < (j + 1) * share, pieces[j], block)
        blocks.append(block)
    return blocks


def correlation_kernel(ports, e, m, ae, cells, amplitude, packed, base, stage, sems):
    _, _, depth, rows, width = e.shape
    share = width // ports
    groups = depth // PLANES
    tile = lax.axis_index("tile")
    plane_cells = lax.axis_size("tile") * rows * width
    target = cells[0] - tile * (rows * width)
    position = row_iota((rows, width)) * width + lane_iota((rows, width))

    def at(ref, c, z):
        return ref[0, c, z] if z < depth else jnp.zeros((rows, width), jnp.float32)

    zero = jnp.zeros((rows, width), jnp.float32)
    fx_prev, fy_prev = zero, zero
    sums_a, sums_b, copies = [], [], []
    for z in range(depth):
        ex, ey, ez = (at(e, c, z) for c in range(3))
        fx = at(m, 0, z) - TIMESTEP * ((lane_next(ez) - ez) - (at(e, 1, z + 1) - ey))
        fy = at(m, 1, z) - TIMESTEP * ((at(e, 0, z + 1) - ex) - (row_next(ez, 0.0) - ez))
        fz = at(m, 2, z) - TIMESTEP * ((row_next(ey, 0.0) - ey) - (lane_next(ex) - ex))
        hit = position == target - z * plane_cells
        drive_x = ((fz - lane_prev(fz)) - (fy - fy_prev)) - jnp.where(hit, amplitude[0, 0], 0.0)
        drive_y = ((fx - fx_prev) - (fz - row_prev(fz, 0.0))) - jnp.where(hit, amplitude[0, 1], 0.0)
        drive_z = ((fy - row_prev(fy, 0.0)) - (fx - lane_prev(fx))) - jnp.where(
            hit, amplitude[0, 2], 0.0
        )
        ax, ay, az = (at(ae, c, z) for c in range(3))
        sums_a.append(ax * ex + ay * ey + az * ez)
        sums_b.append(ax * drive_x + ay * drive_y + az * drive_z)
        fx_prev, fy_prev = fx, fy
        if z % PLANES == PLANES - 1:
            group = z // PLANES
            for f, sums in enumerate((sums_a, sums_b)):
                slab = f * (depth // PLANES) + group
                for port, block in enumerate(pack(sums, share, ports)):
                    stage[port, slab] = block
                    if f == 1:
                        base[port, group : group + 1] = block[:1]
                        base[port, groups + group : groups + group + 1] = block[rows - 1 :]
                copies.append(pltpu.make_async_copy(stage.at[:, slab], packed.at[:, slab], sems.at[slab]))
                copies[-1].start()
            sums_a, sums_b = [], []
    for copy in copies:
        copy.wait()


def rim_kernel(ports, behind, ahead, ae_last, ae_first, e_first, base, packed, patched, stage, sems):
    del packed
    depth = behind.shape[0] // 4
    width = behind.shape[1]
    rows = patched.shape[2]
    groups = depth // PLANES
    share = width // ports
    inside = jnp.where(lax.axis_index("tile") > 0, 1.0, 0.0)

    def part(ref, i):
        return ref[i * depth : (i + 1) * depth, :]

    at_y, at_z = TIMESTEP * part(ahead, 1), -TIMESTEP * part(ahead, 0)
    plane_before = jnp.concatenate([jnp.zeros((1, width), jnp.float32), at_y[:-1]], axis=0)
    drive_x = (at_z - lane_prev(at_z)) - (at_y - plane_before)
    ax, ay, az = (ae_last[c, :depth] for c in range(3))
    last = ax * drive_x - ay * at_z + az * at_y
    prev_y = inside * (part(behind, 0) + TIMESTEP * e_first[1, :depth])
    prev_z = inside * (part(behind, 1) - TIMESTEP * e_first[0, :depth])
    first = ae_first[0, :depth] * prev_z - ae_first[1, :depth] * prev_y
    planes = [
        jnp.concatenate(
            [side[g * PLANES + j : g * PLANES + j + 1] for side in (first, last) for g in range(groups)], axis=0
        )
        for j in range(PLANES)
    ]
    for port, block in enumerate(pack(planes, share, ports)):
        stage[port] = base[port, : 2 * groups] + block
    copies = [
        pltpu.make_async_copy(
            stage.at[:, side * groups + g], patched.at[:, groups + g, side * (rows - 1)], sems.at[side * groups + g]
        )
        for side in range(2)
        for g in range(groups)
    ]
    for copy in copies:
        copy.start()
    for copy in copies:
        copy.wait()


def share_factors(ports, labels, perm, cond, factors):
    depth, rows, width = labels.shape
    share = width // ports
    begin = lax.axis_index("port") * share
    perms, conds = region_values(perm, cond)
    denominators = [p + HALF_STEP * c for p, c in zip(perms, conds, strict=True)]
    scales = [TIMESTEP / (d * d) for d in denominators]
    lane = lane_iota((rows, LANES))
    for group in range(depth // PLANES):
        mine = None
        for j in range(PLANES - 1, -1, -1):
            shift = lax.rem(width - begin + j * share, width)
            piece = pltpu.roll(labels[group * PLANES + j], shift, 1)[:, :LANES]
            mine = piece if mine is None else jnp.where(lane < (j + 1) * share, piece, mine)
        for i, entries in enumerate((scales, perms, conds)):
            factors[i, group] = look_up(mine, entries)


def field_kernel(ports, ae, am, labels, behind, ahead, perm, cond, new_e, new_m, factors):
    depth, rows, width = labels.shape
    share_factors(ports, labels, perm, cond, factors)
    source, update = gains(perm, cond, width)
    above, below = line_of(behind), line_of(ahead)
    inside = jnp.where(lax.axis_index("tile") > 0, 1.0, 0.0)
    zero = jnp.zeros((rows, width), jnp.float32)

    def scaled(z):
        if z == depth:
            return [zero] * 3
        gain = look_up(labels[z], source)
        return [gain * ae[0, c, z] for c in range(3)]

    nx_prev, ny_prev = zero, zero
    here = scaled(0)
    for z in range(depth):
        after = scaled(z + 1)
        sx, sy, sz = here
        next_y = below(2 * depth + z)
        next_z = below(3 * depth + z)
        nx = am[0, 0, z] + ((lane_next(sz) - sz) - (after[1] - sy))
        ny = am[0, 1, z] + ((after[0] - sx) - (row_next(sz, next_z) - sz))
        nz = am[0, 2, z] + ((row_next(sy, next_y) - sy) - (lane_next(sx) - sx))
        prev_y = inside * (above(2 * depth + z) - sz[0:1])
        prev_z = inside * (above(3 * depth + z) + sy[0:1])
        new_m[0, 0, z] = nx
        new_m[0, 1, z] = ny
        new_m[0, 2, z] = nz
        gain = look_up(labels[z], update)
        new_e[0, 0, z] = gain * ae[0, 0, z] - TIMESTEP * ((nz - lane_prev(nz)) - (ny - ny_prev))
        new_e[0, 1, z] = gain * ae[0, 1, z] - TIMESTEP * ((nx - nx_prev) - (nz - row_prev(nz, prev_z)))
        new_e[0, 2, z] = gain * ae[0, 2, z] - TIMESTEP * ((ny - row_prev(ny, prev_y)) - (nx - lane_prev(nx)))
        nx_prev, ny_prev = nx, ny
        here = after


def gradient_kernel(gathered, factors, grad_perm, grad_cond):
    ports, slabs, rows, _ = gathered.shape
    depth, _, share = grad_perm.shape
    groups = depth // PLANES
    sums = []
    for slab in range(slabs):
        total = gathered[0, slab]
        for port in range(1, ports):
            total = total + gathered[port, slab]
        sums.append(total)
    for group in range(groups):
        corr_a, corr_b = sums[group], sums[groups + group]
        factor, permittivity, conductivity = (factors[i, group] for i in range(3))
        by_perm = factor * (conductivity * corr_a - corr_b)
        by_cond = factor * (-permittivity * corr_a - HALF_STEP * corr_b)
        for j in range(PLANES):
            for ref, value in ((grad_perm, by_perm), (grad_cond, by_cond)):
                moved = pltpu.roll(value, LANES - j * share, 1) if j else value
                ref[group * PLANES + j] = moved[:, :share]


def call(kernel, inputs, spaces, outs, out_spaces, flops, moved, scratch=(), aliases=()):
    inputs = [pltpu.with_memory_space_constraint(x, space) if space in (VMEM, HBM) else x for x, space in zip(inputs, spaces, strict=True)]
    return pl.pallas_call(
        kernel,
        out_shape=tuple(space(out.shape, out.dtype) if space in (VMEM, HBM) else out for out, space in zip(outs, out_spaces, strict=True)),
        in_specs=[pl.BlockSpec(memory_space=VMEM if space is HBM_BLOCK else space) for space in spaces],
        out_specs=tuple(pl.BlockSpec(memory_space=VMEM if space is HBM_BLOCK else space) for space in out_spaces),
        scratch_shapes=scratch,
        input_output_aliases=dict(aliases),
        compiler_params=pltpu.CompilerParams(vmem_limit_bytes=VMEM_LIMIT),
        cost_estimate=pl.CostEstimate(flops=flops, bytes_accessed=moved, transcendentals=0),
    )(*inputs)


def on_device(
    electric,
    magnetic,
    adjoint_electric,
    adjoint_magnetic,
    region_labels,
    permittivity_table,
    conductivity_table,
    port_cells,
    port_amplitude,
):
    depth, rows, width = region_labels.shape
    ports = lax.axis_size("port")
    share = width // ports
    cells = depth * rows * width

    def array(*shape):
        return jax.ShapeDtypeStruct(shape, jnp.float32)

    edge = array(4 * depth, width)
    to_ahead, to_behind, *kept = call(
        edge_kernel,
        (electric, magnetic, adjoint_electric, adjoint_magnetic, region_labels, permittivity_table, conductivity_table),
        (HBM,) * 7,
        (edge, edge) + tuple(array(count, EDGE, width) for count in (3, 2, 2)),
        (VMEM,) * 5,
        10 * cells,
        cells * 4 * 14,
        [SMEM(permittivity_table.shape, jnp.float32)] * 2 + [
            VMEM((count, EDGE, width), jnp.float32) for count in (3, 2, 2)
        ] + [VMEM((2, EDGE, width), jnp.int32), pltpu.SemaphoreType.DMA((10,))],
    )
    behind = from_behind(to_ahead, "tile", 1)
    ahead = from_behind(to_behind, "tile", -1)
    shares = array(ports, 2 * depth // PLANES, rows, LANES)
    sems = pltpu.SemaphoreType.DMA((shares.shape[1],))
    packed, base = call(
        functools.partial(correlation_kernel, ports),
        (electric, magnetic, adjoint_electric, port_cells, port_amplitude),
        (VMEM,) * 3 + (SMEM,) * 2,
        (shares, array(ports, EDGE, LANES)),
        (HBM, VMEM),
        60 * cells,
        cells * 4 * 11,
        [VMEM(shares.shape, jnp.float32), sems],
    )
    (packed,) = call(
        functools.partial(rim_kernel, ports),
        (behind, ahead, *kept, base, packed),
        (VMEM,) * 6 + (HBM,),
        (shares,),
        (HBM,),
        2 * cells,
        cells,
        [VMEM((ports, 2 * depth // PLANES, LANES), jnp.float32), sems],
        {6: 0},
    )
    gathered = lax.all_to_all(packed, "port", 0, 0, tiled=True)
    new_electric, new_magnetic, factors = call(
        functools.partial(field_kernel, ports),
        (adjoint_electric, adjoint_magnetic, region_labels, behind, ahead, permittivity_table, conductivity_table),
        (VMEM, HBM_BLOCK, HBM_BLOCK, VMEM, VMEM) + (SMEM,) * 2,
        (array(1, 3, depth, rows, width), array(1, 3, depth, rows, width), array(3, depth // PLANES, rows, LANES)),
        (HBM_BLOCK, HBM_BLOCK, VMEM),
        80 * cells,
        cells * 4 * 13,
    )
    gradient = array(depth, rows, share)
    gradient_perm, gradient_cond = call(
        gradient_kernel,
        (gathered, factors),
        (VMEM,) * 2,
        (gradient, gradient),
        (HBM_BLOCK,) * 2,
        4 * cells,
        cells * 4 * 3,
    )
    return (new_electric, new_magnetic, gradient_perm, gradient_cond)


def solution(mesh):
    return jax.shard_map(
        on_device,
        mesh=mesh,
        in_specs=(
            P("port", None, None, "tile", None),
            P("port", None, None, "tile", None),
            P("port", None, None, "tile", None),
            P("port", None, None, "tile", None),
            P(None, "tile", None),
            P(),
            P(),
            P("port"),
            P("port", None),
        ),
        out_specs=(
            P("port", None, None, "tile", None),
            P("port", None, None, "tile", None),
            P(None, "tile", "port"),
            P(None, "tile", "port"),
        ),
        check_vma=False,
    )
```

```python
import functools

import jax
import jax.numpy as jnp
from jax import lax
from jax.experimental import pallas as pl
from jax.experimental.pallas import tpu as pltpu
from jax.sharding import PartitionSpec as P

TIMESTEP = 0.5
HALF_STEP = 0.25
PLANES = 3
LANES = 128
EDGE = 8
VMEM_LIMIT = 12 << 20
VMEM = pltpu.VMEM
SMEM = pltpu.SMEM
HBM = pltpu.HBM
HBM_BLOCK = None


def from_behind(value, axis, steps):
    count = lax.axis_size(axis)
    first, last = (max(0, -steps), min(count, count - steps))
    return lax.ppermute(value, axis, [(source, source + steps) for source in range(first, last)])


def lane_iota(shape):
    return lax.broadcasted_iota(jnp.int32, shape, len(shape) - 1)


def row_iota(shape):
    return lax.broadcasted_iota(jnp.int32, shape, len(shape) - 2)


def lane_next(value):
    width = value.shape[1]
    return jnp.where(lane_iota(value.shape) == width - 1, 0.0, pltpu.roll(value, width - 1, 1))


def lane_prev(value):
    return jnp.where(lane_iota(value.shape) == 0, 0.0, pltpu.roll(value, 1, 1))


def row_next(value, beyond):
    rows = value.shape[0]
    return jnp.where(row_iota(value.shape) == rows - 1, beyond, pltpu.roll(value, rows - 1, 0))


def row_prev(value, before):
    return jnp.where(row_iota(value.shape) == 0, before, pltpu.roll(value, 1, 0))


def look_up(labels, entries):
    count = len(entries)
    level = list(entries)
    bit = 1
    while len(level) > 1:
        odd = (labels & bit) != 0
        level = [
            jnp.where(odd, level[i + 1], level[i]) if i + 1 < len(level) else level[i]
            for i in range(0, len(level), 2)
        ]
        bit *= 2
    assert count <= bit
    return level[0]


def region_values(perm_ref, cond_ref):
    shape = (1, LANES)
    perm = [jnp.full(shape, perm_ref[r], jnp.float32) for r in range(perm_ref.shape[0])]
    cond = [jnp.full(shape, cond_ref[r], jnp.float32) for r in range(cond_ref.shape[0])]
    return perm, cond


def widen(entries, width):
    return [jnp.concatenate([entry] * (width // LANES), axis=1) for entry in entries]


def gains(perm_ref, cond_ref, width):
    perm, cond = region_values(perm_ref, cond_ref)
    denominator = [p + HALF_STEP * c for p, c in zip(perm, cond, strict=True)]
    source = [TIMESTEP / d for d in denominator]
    update = [(p - HALF_STEP * c) / d for p, c, d in zip(perm, cond, denominator, strict=True)]
    return widen(source, width), widen(update, width)


def edge_kernel(e, m, ae, am, labels, perms, conds, amplitude, to_ahead, to_behind, ae_last, ae_first, e_first, push, perm, cond, force, e_last, m_last, am_last, marks, sems):
    _, _, depth, rows, width = e.shape
    last = rows - 1
    planes = pl.ds(0, depth)
    for ref in (ae_last, ae_first, e_first, e_last, m_last, am_last):
        ref[:, depth:, :] = jnp.zeros((ref.shape[0], EDGE - depth, width), jnp.float32)
    moves = (
        (perms, perm),
        (conds, cond),
        (amplitude, force),
        (ae.at[0, :, :, last], ae_last.at[:, planes]),
        (ae.at[0, pl.ds(1, 2), :, 0], ae_first.at[:, planes]),
        (labels.at[:, last], marks.at[0, planes]),
        (labels.at[:, 0], marks.at[1, planes]),
        (e.at[0, :, :, last], e_last.at[:, planes]),
        (e.at[0, pl.ds(1, 2), :, 0], e_first.at[:, planes]),
        (m.at[0, pl.ds(1, 2), :, last], m_last.at[:, planes]),
        (am.at[0, pl.ds(1, 2), :, last], am_last.at[:, planes]),
    )
    copies = [pltpu.make_async_copy(src, dst, sems.at[i]) for i, (src, dst) in enumerate(moves)]
    for copy in copies:
        copy.start()
    def plane_next(value):
        return pltpu.roll(value, EDGE - 1, 0)

    for copy in copies:
        copy.wait()
    source, _ = gains(perm, cond, width)
    for c in range(3):
        push[c] = jnp.full(push.shape[1:], force[0, c], jnp.float32)
    last_gain, first_gain = (look_up(marks[i], source) for i in range(2))
    ex, ey, ez = (e_last[c] for c in range(3))
    sx, sy, sz = (last_gain * ae_last[c] for c in range(3))
    up = (
        m_last[0] - TIMESTEP * ((plane_next(ex) - ex) + ez),
        m_last[1] + TIMESTEP * (ey + (lane_next(ex) - ex)),
        am_last[0] + ((plane_next(sx) - sx) + sz),
        am_last[1] - (sy + (lane_next(sx) - sx)),
    )
    down = (e_first[0], e_first[1], first_gain * ae_first[0], first_gain * ae_first[1])
    for i, (above, below) in enumerate(zip(up, down, strict=True)):
        at = i * depth
        to_ahead[at : at + depth, :] = above[:depth]
        to_behind[at : at + depth, :] = below[:depth]


def line_of(ref):
    return lambda i: ref[i : i + 1, :]


def pack(planes, share, ports):
    rows = planes[0].shape[0]
    lane = lane_iota((rows, LANES))
    blocks = []
    for port in range(ports):
        tile, offset = divmod(port * share, LANES)
        pieces = []
        for j, plane in enumerate(planes):
            piece = plane[:, tile * LANES : (tile + 1) * LANES]
            if offset + share > LANES:
                piece = jnp.where(
                    lane >= offset, piece, plane[:, (tile + 1) * LANES : (tile + 2) * LANES]
                )
            shift = (j * share - offset) % LANES
            pieces.append(pltpu.roll(piece, shift, 1) if shift else piece)
        block = pieces[-1]
        for j in range(len(planes) - 2, -1, -1):
            block = jnp.where(lane < (j + 1) * share, pieces[j], block)
        blocks.append(block)
    return blocks


def drive_shares(ports, e, m, ae, cells, amplitude, drives):
    _, _, depth, rows, width = e.shape
    share = width // ports
    tile = lax.axis_index("tile")
    plane_cells = lax.axis_size("tile") * rows * width
    target = cells[0] - tile * (rows * width)
    push = [jnp.concatenate([amplitude[c, :1]] * (width // LANES), axis=1) for c in range(3)]
    position = row_iota((rows, width)) * width + lane_iota((rows, width))

    def at(ref, c, z):
        return ref[0, c, z] if z < depth else jnp.zeros((rows, width), jnp.float32)

    zero = jnp.zeros((rows, width), jnp.float32)
    fx_prev, fy_prev = zero, zero
    sums = []
    for z in range(depth):
        ex, ey, ez = (at(e, c, z) for c in range(3))
        fx = at(m, 0, z) - TIMESTEP * ((lane_next(ez) - ez) - (at(e, 1, z + 1) - ey))
        fy = at(m, 1, z) - TIMESTEP * ((at(e, 0, z + 1) - ex) - (row_next(ez, 0.0) - ez))
        fz = at(m, 2, z) - TIMESTEP * ((row_next(ey, 0.0) - ey) - (lane_next(ex) - ex))
        hit = position == target - z * plane_cells
        drive_x = ((fz - lane_prev(fz)) - (fy - fy_prev)) - jnp.where(hit, push[0], 0.0)
        drive_y = ((fx - fx_prev) - (fz - row_prev(fz, 0.0))) - jnp.where(hit, push[1], 0.0)
        drive_z = ((fy - row_prev(fy, 0.0)) - (fx - lane_prev(fx))) - jnp.where(
            hit, push[2], 0.0
        )
        ax, ay, az = (at(ae, c, z) for c in range(3))
        sums.append(ax * drive_x + ay * drive_y + az * drive_z)
        fx_prev, fy_prev = fx, fy
        if z % PLANES == PLANES - 1:
            for port, block in enumerate(pack(sums, share, ports)):
                drives[port, z // PLANES] = block
            sums = []


def at_seam():
    return lax.axis_index("tile") == lax.axis_size("tile") // 2


def electric_shares(ports, e, ae, packed, stage, sems):
    _, _, depth, _, width = e.shape
    groups = depth // PLANES
    copies = []
    for group in range(groups):
        planes = []
        for z in range(group * PLANES, (group + 1) * PLANES):
            ax, ay, az = (ae[0, c, z] for c in range(3))
            planes.append(ax * e[0, 0, z] + ay * e[0, 1, z] + az * e[0, 2, z])
        for port, block in enumerate(pack(planes, width // ports, ports)):
            stage[port, group] = block
        copies.append(pltpu.make_async_copy(stage.at[:, group], packed.at[:, group], sems.at[group]))
        copies[-1].start()
    return copies


def early_kernel(ports, e, ae, edge, packed, edge_out, stage, sems):
    del edge, edge_out

    @pl.when(at_seam())
    def _():
        for copy in electric_shares(ports, e, ae, packed, stage, sems):
            copy.wait()


def late_kernel(ports, e, m, ae, cells, amplitude, packed_in, packed, drives, stage, sems):
    del packed_in

    @pl.when(jnp.logical_not(at_seam()))
    def _():
        copies = electric_shares(ports, e, ae, packed, stage, sems)
        drive_shares(ports, e, m, ae, cells, amplitude, drives)
        for copy in copies:
            copy.wait()

    @pl.when(at_seam())
    def _():
        drive_shares(ports, e, m, ae, cells, amplitude, drives)


def rim_kernel(ports, behind, ahead, ae_last, ae_first, e_first, drives_in, packed, drives, patched, sem):
    del drives_in, packed
    depth = behind.shape[0] // 4
    width = behind.shape[1]
    rows = patched.shape[2]
    groups = depth // PLANES
    share = width // ports
    inside = jnp.where(lax.axis_index("tile") > 0, 1.0, 0.0)

    def part(ref, i):
        return ref[i * depth : (i + 1) * depth, :]

    at_y, at_z = TIMESTEP * part(ahead, 1), -TIMESTEP * part(ahead, 0)
    plane_before = jnp.concatenate([jnp.zeros((1, width), jnp.float32), at_y[:-1]], axis=0)
    drive_x = (at_z - lane_prev(at_z)) - (at_y - plane_before)
    ax, ay, az = (ae_last[c, :depth] for c in range(3))
    last = ax * drive_x - ay * at_z + az * at_y
    prev_y = inside * (part(behind, 0) + TIMESTEP * e_first[1, :depth])
    prev_z = inside * (part(behind, 1) - TIMESTEP * e_first[0, :depth])
    first = ae_first[0, :depth] * prev_z - ae_first[1, :depth] * prev_y
    planes = [
        jnp.concatenate(
            [side[g * PLANES + j : g * PLANES + j + 1] for side in (first, last) for g in range(groups)], axis=0
        )
        for j in range(PLANES)
    ]
    for port, block in enumerate(pack(planes, share, ports)):
        for g in range(groups):
            drives[port, g, :1] = drives[port, g, :1] + block[g : g + 1]
            drives[port, g, rows - 1 :] = drives[port, g, rows - 1 :] + block[groups + g : groups + g + 1]
    copy = pltpu.make_async_copy(drives, patched.at[:, pl.ds(groups, groups)], sem.at[0])
    copy.start()
    copy.wait()


def share_factors(ports, labels, perm, cond, factors):
    depth, rows, width = labels.shape
    share = width // ports
    begin = lax.axis_index("port") * share
    perms, conds = region_values(perm, cond)
    denominators = [p + HALF_STEP * c for p, c in zip(perms, conds, strict=True)]
    scales = [TIMESTEP / (d * d) for d in denominators]
    lane = lane_iota((rows, LANES))
    for group in range(depth // PLANES):
        mine = None
        for j in range(PLANES - 1, -1, -1):
            shift = lax.rem(width - begin + j * share, width)
            piece = pltpu.roll(labels[group * PLANES + j], shift, 1)[:, :LANES]
            mine = piece if mine is None else jnp.where(lane < (j + 1) * share, piece, mine)
        for i, entries in enumerate((scales, perms, conds)):
            factors[i, group] = look_up(mine, entries)


def field_kernel(ports, ae, am, labels, behind, ahead, perm, cond, new_e, new_m, factors):
    depth, rows, width = labels.shape
    share_factors(ports, labels, perm, cond, factors)
    source, update = gains(perm, cond, width)
    above, below = line_of(behind), line_of(ahead)
    inside = jnp.where(lax.axis_index("tile") > 0, 1.0, 0.0)
    zero = jnp.zeros((rows, width), jnp.float32)

    def scaled(z):
        if z == depth:
            return [zero] * 3
        gain = look_up(labels[z], source)
        return [gain * ae[0, c, z] for c in range(3)]

    nx_prev, ny_prev = zero, zero
    here = scaled(0)
    for z in range(depth):
        after = scaled(z + 1)
        sx, sy, sz = here
        next_y = below(2 * depth + z)
        next_z = below(3 * depth + z)
        nx = am[0, 0, z] + ((lane_next(sz) - sz) - (after[1] - sy))
        ny = am[0, 1, z] + ((after[0] - sx) - (row_next(sz, next_z) - sz))
        nz = am[0, 2, z] + ((row_next(sy, next_y) - sy) - (lane_next(sx) - sx))
        prev_y = inside * (above(2 * depth + z) - sz[0:1])
        prev_z = inside * (above(3 * depth + z) + sy[0:1])
        new_m[0, 0, z] = nx
        new_m[0, 1, z] = ny
        new_m[0, 2, z] = nz
        gain = look_up(labels[z], update)
        new_e[0, 0, z] = gain * ae[0, 0, z] - TIMESTEP * ((nz - lane_prev(nz)) - (ny - ny_prev))
        new_e[0, 1, z] = gain * ae[0, 1, z] - TIMESTEP * ((nx - nx_prev) - (nz - row_prev(nz, prev_z)))
        new_e[0, 2, z] = gain * ae[0, 2, z] - TIMESTEP * ((ny - row_prev(ny, prev_y)) - (nx - lane_prev(nx)))
        nx_prev, ny_prev = nx, ny
        here = after


def gradient_kernel(gathered, factors, grad_perm, grad_cond):
    ports, slabs, rows, _ = gathered.shape
    depth, _, share = grad_perm.shape
    groups = depth // PLANES
    sums = []
    for slab in range(slabs):
        total = gathered[0, slab]
        for port in range(1, ports):
            total = total + gathered[port, slab]
        sums.append(total)
    for group in range(groups):
        corr_a, corr_b = sums[group], sums[groups + group]
        factor, permittivity, conductivity = (factors[i, group] for i in range(3))
        by_perm = factor * (conductivity * corr_a - corr_b)
        by_cond = factor * (-permittivity * corr_a - HALF_STEP * corr_b)
        for j in range(PLANES):
            for ref, value in ((grad_perm, by_perm), (grad_cond, by_cond)):
                moved = pltpu.roll(value, LANES - j * share, 1) if j else value
                ref[group * PLANES + j] = moved[:, :share]


def call(kernel, inputs, spaces, outs, out_spaces, flops, moved, scratch=(), aliases=()):
    inputs = [pltpu.with_memory_space_constraint(x, space) if space in (VMEM, HBM) else x for x, space in zip(inputs, spaces, strict=True)]
    return pl.pallas_call(
        kernel,
        out_shape=tuple(space(out.shape, out.dtype) if space in (VMEM, HBM) else out for out, space in zip(outs, out_spaces, strict=True)),
        in_specs=[pl.BlockSpec(memory_space=VMEM if space is HBM_BLOCK else space) for space in spaces],
        out_specs=tuple(pl.BlockSpec(memory_space=VMEM if space is HBM_BLOCK else space) for space in out_spaces),
        scratch_shapes=scratch,
        input_output_aliases=dict(aliases),
        compiler_params=pltpu.CompilerParams(vmem_limit_bytes=VMEM_LIMIT),
        cost_estimate=pl.CostEstimate(flops=flops, bytes_accessed=moved, transcendentals=0),
    )(*inputs)


def on_device(
    electric,
    magnetic,
    adjoint_electric,
    adjoint_magnetic,
    region_labels,
    permittivity_table,
    conductivity_table,
    port_cells,
    port_amplitude,
):
    depth, rows, width = region_labels.shape
    ports = lax.axis_size("port")
    share = width // ports
    cells = depth * rows * width

    def array(*shape):
        return jax.ShapeDtypeStruct(shape, jnp.float32)

    edge = array(4 * depth, width)
    to_ahead, to_behind, *kept, push = call(
        edge_kernel,
        (electric, magnetic, adjoint_electric, adjoint_magnetic, region_labels, permittivity_table, conductivity_table, port_amplitude),
        (HBM,) * 8,
        (edge, edge) + tuple(array(count, EDGE, width) for count in (3, 2, 2)) + (array(3, EDGE, LANES),),
        (VMEM,) * 6,
        10 * cells,
        cells * 4 * 14,
        [SMEM(permittivity_table.shape, jnp.float32)] * 2 + [SMEM(port_amplitude.shape, jnp.float32)] + [
            VMEM((count, EDGE, width), jnp.float32) for count in (3, 2, 2)
        ] + [VMEM((2, EDGE, width), jnp.int32), pltpu.SemaphoreType.DMA((11,))],
    )
    behind = from_behind(to_ahead, "tile", 1)
    shares = array(ports, 2 * depth // PLANES, rows, LANES)
    half = array(ports, depth // PLANES, rows, LANES)
    stage = [VMEM(half.shape, jnp.float32), pltpu.SemaphoreType.DMA((half.shape[1],))]
    packed, to_behind = call(
        functools.partial(early_kernel, ports),
        (electric, adjoint_electric, to_behind),
        (VMEM,) * 3,
        (shares, edge),
        (HBM, VMEM),
        cells,
        cells,
        stage,
        {2: 1},
    )
    ahead = from_behind(to_behind, "tile", -1)
    packed, drives = call(
        functools.partial(late_kernel, ports),
        (electric, magnetic, adjoint_electric, port_cells, push, packed),
        (VMEM,) * 3 + (SMEM, VMEM, HBM),
        (shares, half),
        (HBM, VMEM),
        60 * cells,
        cells * 4 * 11,
        stage,
        {5: 0},
    )
    _, packed = call(
        functools.partial(rim_kernel, ports),
        (behind, ahead, *kept, drives, packed),
        (VMEM,) * 6 + (HBM,),
        (half, shares),
        (VMEM, HBM),
        2 * cells,
        cells,
        [pltpu.SemaphoreType.DMA((1,))],
        {5: 0, 6: 1},
    )
    gathered = lax.all_to_all(packed, "port", 0, 0, tiled=True)
    new_electric, new_magnetic, factors = call(
        functools.partial(field_kernel, ports),
        (adjoint_electric, adjoint_magnetic, region_labels, behind, ahead, permittivity_table, conductivity_table),
        (VMEM, HBM_BLOCK, HBM_BLOCK, VMEM, VMEM) + (SMEM,) * 2,
        (array(1, 3, depth, rows, width), array(1, 3, depth, rows, width), array(3, depth // PLANES, rows, LANES)),
        (HBM_BLOCK, HBM_BLOCK, VMEM),
        80 * cells,
        cells * 4 * 13,
    )
    gradient = array(depth, rows, share)
    gradient_perm, gradient_cond = call(
        gradient_kernel,
        (gathered, factors),
        (VMEM,) * 2,
        (gradient, gradient),
        (HBM_BLOCK,) * 2,
        4 * cells,
        cells * 4 * 3,
    )
    return (new_electric, new_magnetic, gradient_perm, gradient_cond)


def solution(mesh):
    return jax.shard_map(
        on_device,
        mesh=mesh,
        in_specs=(
            P("port", None, None, "tile", None),
            P("port", None, None, "tile", None),
            P("port", None, None, "tile", None),
            P("port", None, None, "tile", None),
            P(None, "tile", None),
            P(),
            P(),
            P("port"),
            P("port", None),
        ),
        out_specs=(
            P("port", None, None, "tile", None),
            P("port", None, None, "tile", None),
            P(None, "tile", "port"),
            P(None, "tile", "port"),
        ),
        check_vma=False,
    )
```

```python
import functools

import jax
import jax.numpy as jnp
from jax import lax
from jax.experimental import pallas as pl
from jax.experimental.pallas import tpu as pltpu
from jax.sharding import PartitionSpec as P

TIMESTEP = 0.5
HALF_STEP = 0.25
PLANES = 3
LANES = 128
EDGE = 8
VMEM_LIMIT = 12 << 20
VMEM = pltpu.VMEM
SMEM = pltpu.SMEM
HBM = pltpu.HBM
HBM_BLOCK = None


def from_behind(value, axis, steps):
    count = lax.axis_size(axis)
    first, last = (max(0, -steps), min(count, count - steps))
    return lax.ppermute(value, axis, [(source, source + steps) for source in range(first, last)])


def lane_iota(shape):
    return lax.broadcasted_iota(jnp.int32, shape, len(shape) - 1)


def row_iota(shape):
    return lax.broadcasted_iota(jnp.int32, shape, len(shape) - 2)


def lane_next(value):
    width = value.shape[1]
    return jnp.where(lane_iota(value.shape) == width - 1, 0.0, pltpu.roll(value, width - 1, 1))


def lane_prev(value):
    return jnp.where(lane_iota(value.shape) == 0, 0.0, pltpu.roll(value, 1, 1))


def row_next(value, beyond):
    rows = value.shape[0]
    return jnp.where(row_iota(value.shape) == rows - 1, beyond, pltpu.roll(value, rows - 1, 0))


def row_prev(value, before):
    return jnp.where(row_iota(value.shape) == 0, before, pltpu.roll(value, 1, 0))


def look_up(labels, entries):
    count = len(entries)
    level = list(entries)
    bit = 1
    while len(level) > 1:
        odd = (labels & bit) != 0
        level = [
            jnp.where(odd, level[i + 1], level[i]) if i + 1 < len(level) else level[i]
            for i in range(0, len(level), 2)
        ]
        bit *= 2
    assert count <= bit
    return level[0]


def region_values(perm_ref, cond_ref):
    shape = (1, LANES)
    perm = [jnp.full(shape, perm_ref[r], jnp.float32) for r in range(perm_ref.shape[0])]
    cond = [jnp.full(shape, cond_ref[r], jnp.float32) for r in range(cond_ref.shape[0])]
    return perm, cond


def widen(entries, width):
    return [jnp.concatenate([entry] * (width // LANES), axis=1) for entry in entries]


def gains(perm_ref, cond_ref, width):
    perm, cond = region_values(perm_ref, cond_ref)
    denominator = [p + HALF_STEP * c for p, c in zip(perm, cond, strict=True)]
    source = [TIMESTEP / d for d in denominator]
    update = [(p - HALF_STEP * c) / d for p, c, d in zip(perm, cond, denominator, strict=True)]
    return widen(source, width), widen(update, width)


def edge_kernel(e, m, ae, am, labels, perms, conds, amplitude, to_ahead, to_behind, ae_last, ae_first, e_first, push, perm, cond, force, e_last, m_last, am_last, marks, sems):
    _, _, depth, rows, width = e.shape
    last = rows - 1
    planes = pl.ds(0, depth)
    for ref in (ae_last, ae_first, e_first, e_last, m_last, am_last):
        ref[:, depth:, :] = jnp.zeros((ref.shape[0], EDGE - depth, width), jnp.float32)
    moves = (
        (perms, perm),
        (conds, cond),
        (amplitude, force),
        (ae.at[0, :, :, last], ae_last.at[:, planes]),
        (ae.at[0, pl.ds(1, 2), :, 0], ae_first.at[:, planes]),
        (labels.at[:, last], marks.at[0, planes]),
        (labels.at[:, 0], marks.at[1, planes]),
        (e.at[0, :, :, last], e_last.at[:, planes]),
        (e.at[0, pl.ds(1, 2), :, 0], e_first.at[:, planes]),
        (m.at[0, pl.ds(1, 2), :, last], m_last.at[:, planes]),
        (am.at[0, pl.ds(1, 2), :, last], am_last.at[:, planes]),
    )
    copies = [pltpu.make_async_copy(src, dst, sems.at[i]) for i, (src, dst) in enumerate(moves)]
    for copy in copies:
        copy.start()
    def plane_next(value):
        return pltpu.roll(value, EDGE - 1, 0)

    for copy in copies:
        copy.wait()
    source, _ = gains(perm, cond, width)
    for c in range(3):
        push[c] = jnp.full(push.shape[1:], force[0, c], jnp.float32)
    last_gain, first_gain = (look_up(marks[i], source) for i in range(2))
    ex, ey, ez = (e_last[c] for c in range(3))
    sx, sy, sz = (last_gain * ae_last[c] for c in range(3))
    up = (
        m_last[0] - TIMESTEP * ((plane_next(ex) - ex) + ez),
        m_last[1] + TIMESTEP * (ey + (lane_next(ex) - ex)),
        am_last[0] + ((plane_next(sx) - sx) + sz),
        am_last[1] - (sy + (lane_next(sx) - sx)),
    )
    down = (e_first[0], e_first[1], first_gain * ae_first[0], first_gain * ae_first[1])
    for i, (above, below) in enumerate(zip(up, down, strict=True)):
        at = i * depth
        to_ahead[at : at + depth, :] = above[:depth]
        to_behind[at : at + depth, :] = below[:depth]


def line_of(ref):
    return lambda i: ref[i : i + 1, :]


def pack(planes, share, ports):
    rows = planes[0].shape[0]
    lane = lane_iota((rows, LANES))
    blocks = []
    for port in range(ports):
        tile, offset = divmod(port * share, LANES)
        pieces = []
        for j, plane in enumerate(planes):
            piece = plane[:, tile * LANES : (tile + 1) * LANES]
            if offset + share > LANES:
                piece = jnp.where(
                    lane >= offset, piece, plane[:, (tile + 1) * LANES : (tile + 2) * LANES]
                )
            shift = (j * share - offset) % LANES
            pieces.append(pltpu.roll(piece, shift, 1) if shift else piece)
        block = pieces[-1]
        for j in range(len(planes) - 2, -1, -1):
            block = jnp.where(lane < (j + 1) * share, pieces[j], block)
        blocks.append(block)
    return blocks


def drive_shares(ports, e, m, ae, cells, amplitude, drives):
    _, _, depth, rows, width = e.shape
    share = width // ports
    tile = lax.axis_index("tile")
    plane_cells = lax.axis_size("tile") * rows * width
    target = cells[0] - tile * (rows * width)
    push = [jnp.concatenate([amplitude[c, :1]] * (width // LANES), axis=1) for c in range(3)]
    position = row_iota((rows, width)) * width + lane_iota((rows, width))

    def at(ref, c, z):
        return ref[0, c, z] if z < depth else jnp.zeros((rows, width), jnp.float32)

    zero = jnp.zeros((rows, width), jnp.float32)
    fx_prev, fy_prev = zero, zero
    sums = []
    for z in range(depth):
        ex, ey, ez = (at(e, c, z) for c in range(3))
        fx = at(m, 0, z) - TIMESTEP * ((lane_next(ez) - ez) - (at(e, 1, z + 1) - ey))
        fy = at(m, 1, z) - TIMESTEP * ((at(e, 0, z + 1) - ex) - (row_next(ez, 0.0) - ez))
        fz = at(m, 2, z) - TIMESTEP * ((row_next(ey, 0.0) - ey) - (lane_next(ex) - ex))
        hit = position == target - z * plane_cells
        drive_x = ((fz - lane_prev(fz)) - (fy - fy_prev)) - jnp.where(hit, push[0], 0.0)
        drive_y = ((fx - fx_prev) - (fz - row_prev(fz, 0.0))) - jnp.where(hit, push[1], 0.0)
        drive_z = ((fy - row_prev(fy, 0.0)) - (fx - lane_prev(fx))) - jnp.where(
            hit, push[2], 0.0
        )
        ax, ay, az = (at(ae, c, z) for c in range(3))
        sums.append(ax * drive_x + ay * drive_y + az * drive_z)
        fx_prev, fy_prev = fx, fy
        if z % PLANES == PLANES - 1:
            for port, block in enumerate(pack(sums, share, ports)):
                drives[port, z // PLANES] = block
            sums = []


def at_seam():
    return lax.axis_index("tile") == lax.axis_size("tile") // 2


def electric_shares(ports, e, ae, packed, stage, sems):
    _, _, depth, _, width = e.shape
    groups = depth // PLANES
    copies = []
    for group in range(groups):
        planes = []
        for z in range(group * PLANES, (group + 1) * PLANES):
            ax, ay, az = (ae[0, c, z] for c in range(3))
            planes.append(ax * e[0, 0, z] + ay * e[0, 1, z] + az * e[0, 2, z])
        for port, block in enumerate(pack(planes, width // ports, ports)):
            stage[port, group] = block
        copies.append(pltpu.make_async_copy(stage.at[:, group], packed.at[:, group], sems.at[group]))
        copies[-1].start()
    return copies


def early_kernel(ports, e, ae, edge, packed, edge_out, stage, sems):
    edge_out[...] = edge[...]

    @pl.when(at_seam())
    def _():
        for copy in electric_shares(ports, e, ae, packed, stage, sems):
            copy.wait()


def late_kernel(ports, e, m, ae, cells, amplitude, packed_in, packed, drives, stage, sems):
    del packed_in

    @pl.when(jnp.logical_not(at_seam()))
    def _():
        copies = electric_shares(ports, e, ae, packed, stage, sems)
        drive_shares(ports, e, m, ae, cells, amplitude, drives)
        for copy in copies:
            copy.wait()

    @pl.when(at_seam())
    def _():
        drive_shares(ports, e, m, ae, cells, amplitude, drives)


def rim_kernel(ports, behind, ahead, ae_last, ae_first, e_first, drives, packed, patched, stage, sems):
    del packed
    depth = behind.shape[0] // 4
    width = behind.shape[1]
    rows = patched.shape[2]
    groups = depth // PLANES
    share = width // ports
    inside = jnp.where(lax.axis_index("tile") > 0, 1.0, 0.0)

    def part(ref, i):
        return ref[i * depth : (i + 1) * depth, :]

    at_y, at_z = TIMESTEP * part(ahead, 1), -TIMESTEP * part(ahead, 0)
    plane_before = jnp.concatenate([jnp.zeros((1, width), jnp.float32), at_y[:-1]], axis=0)
    drive_x = (at_z - lane_prev(at_z)) - (at_y - plane_before)
    ax, ay, az = (ae_last[c, :depth] for c in range(3))
    last = ax * drive_x - ay * at_z + az * at_y
    prev_y = inside * (part(behind, 0) + TIMESTEP * e_first[1, :depth])
    prev_z = inside * (part(behind, 1) - TIMESTEP * e_first[0, :depth])
    first = ae_first[0, :depth] * prev_z - ae_first[1, :depth] * prev_y
    planes = [
        jnp.concatenate(
            [side[g * PLANES + j : g * PLANES + j + 1] for side in (first, last) for g in range(groups)], axis=0
        )
        for j in range(PLANES)
    ]
    blocks = pack(planes, share, ports)
    row = row_iota((rows, LANES))
    copies = []
    for g in range(groups):
        for port, block in enumerate(blocks):
            edges = jnp.where(row == 0, block[g : g + 1], block[groups + g : groups + g + 1])
            inner = jnp.logical_and(row > 0, row < rows - 1)
            stage[port, g] = drives[port, g] + jnp.where(inner, 0.0, edges)
        copies.append(pltpu.make_async_copy(stage.at[:, g], patched.at[:, groups + g], sems.at[g]))
        copies[-1].start()
    for copy in copies:
        copy.wait()


def share_factors(ports, labels, perm, cond, factors):
    depth, rows, width = labels.shape
    share = width // ports
    begin = lax.axis_index("port") * share
    perms, conds = region_values(perm, cond)
    denominators = [p + HALF_STEP * c for p, c in zip(perms, conds, strict=True)]
    scales = [TIMESTEP / (d * d) for d in denominators]
    lane = lane_iota((rows, LANES))
    for group in range(depth // PLANES):
        mine = None
        for j in range(PLANES - 1, -1, -1):
            shift = lax.rem(width - begin + j * share, width)
            piece = pltpu.roll(labels[group * PLANES + j], shift, 1)[:, :LANES]
            mine = piece if mine is None else jnp.where(lane < (j + 1) * share, piece, mine)
        for i, entries in enumerate((scales, perms, conds)):
            factors[i, group] = look_up(mine, entries)


def field_kernel(ports, ae, am, labels, behind, ahead, perm, cond, new_e, new_m, factors):
    depth, rows, width = labels.shape
    share_factors(ports, labels, perm, cond, factors)
    source, update = gains(perm, cond, width)
    above, below = line_of(behind), line_of(ahead)
    inside = jnp.where(lax.axis_index("tile") > 0, 1.0, 0.0)
    zero = jnp.zeros((rows, width), jnp.float32)

    def scaled(z):
        if z == depth:
            return [zero] * 3
        gain = look_up(labels[z], source)
        return [gain * ae[0, c, z] for c in range(3)]

    nx_prev, ny_prev = zero, zero
    here = scaled(0)
    for z in range(depth):
        after = scaled(z + 1)
        sx, sy, sz = here
        next_y = below(2 * depth + z)
        next_z = below(3 * depth + z)
        nx = am[0, 0, z] + ((lane_next(sz) - sz) - (after[1] - sy))
        ny = am[0, 1, z] + ((after[0] - sx) - (row_next(sz, next_z) - sz))
        nz = am[0, 2, z] + ((row_next(sy, next_y) - sy) - (lane_next(sx) - sx))
        prev_y = inside * (above(2 * depth + z) - sz[0:1])
        prev_z = inside * (above(3 * depth + z) + sy[0:1])
        new_m[0, 0, z] = nx
        new_m[0, 1, z] = ny
        new_m[0, 2, z] = nz
        gain = look_up(labels[z], update)
        new_e[0, 0, z] = gain * ae[0, 0, z] - TIMESTEP * ((nz - lane_prev(nz)) - (ny - ny_prev))
        new_e[0, 1, z] = gain * ae[0, 1, z] - TIMESTEP * ((nx - nx_prev) - (nz - row_prev(nz, prev_z)))
        new_e[0, 2, z] = gain * ae[0, 2, z] - TIMESTEP * ((ny - row_prev(ny, prev_y)) - (nx - lane_prev(nx)))
        nx_prev, ny_prev = nx, ny
        here = after


def gradient_kernel(gathered, factors, grad_perm, grad_cond):
    ports, slabs, rows, _ = gathered.shape
    depth, _, share = grad_perm.shape
    groups = depth // PLANES
    sums = []
    for slab in range(slabs):
        total = gathered[0, slab]
        for port in range(1, ports):
            total = total + gathered[port, slab]
        sums.append(total)
    for group in range(groups):
        corr_a, corr_b = sums[group], sums[groups + group]
        factor, permittivity, conductivity = (factors[i, group] for i in range(3))
        by_perm = factor * (conductivity * corr_a - corr_b)
        by_cond = factor * (-permittivity * corr_a - HALF_STEP * corr_b)
        for j in range(PLANES):
            for ref, value in ((grad_perm, by_perm), (grad_cond, by_cond)):
                moved = pltpu.roll(value, LANES - j * share, 1) if j else value
                ref[group * PLANES + j] = moved[:, :share]


def call(kernel, inputs, spaces, outs, out_spaces, flops, moved, scratch=(), aliases=()):
    inputs = [pltpu.with_memory_space_constraint(x, space) if space in (VMEM, HBM) else x for x, space in zip(inputs, spaces, strict=True)]
    return pl.pallas_call(
        kernel,
        out_shape=tuple(space(out.shape, out.dtype) if space in (VMEM, HBM) else out for out, space in zip(outs, out_spaces, strict=True)),
        in_specs=[pl.BlockSpec(memory_space=VMEM if space is HBM_BLOCK else space) for space in spaces],
        out_specs=tuple(pl.BlockSpec(memory_space=VMEM if space is HBM_BLOCK else space) for space in out_spaces),
        scratch_shapes=scratch,
        input_output_aliases=dict(aliases),
        compiler_params=pltpu.CompilerParams(vmem_limit_bytes=VMEM_LIMIT),
        cost_estimate=pl.CostEstimate(flops=flops, bytes_accessed=moved, transcendentals=0),
    )(*inputs)


def on_device(
    electric,
    magnetic,
    adjoint_electric,
    adjoint_magnetic,
    region_labels,
    permittivity_table,
    conductivity_table,
    port_cells,
    port_amplitude,
):
    depth, rows, width = region_labels.shape
    ports = lax.axis_size("port")
    share = width // ports
    cells = depth * rows * width

    def array(*shape):
        return jax.ShapeDtypeStruct(shape, jnp.float32)

    edge = array(4 * depth, width)
    to_ahead, to_behind, *kept, push = call(
        edge_kernel,
        (electric, magnetic, adjoint_electric, adjoint_magnetic, region_labels, permittivity_table, conductivity_table, port_amplitude),
        (HBM,) * 8,
        (edge, edge) + tuple(array(count, EDGE, width) for count in (3, 2, 2)) + (array(3, EDGE, LANES),),
        (VMEM,) * 6,
        10 * cells,
        cells * 4 * 14,
        [SMEM(permittivity_table.shape, jnp.float32)] * 2 + [SMEM(port_amplitude.shape, jnp.float32)] + [
            VMEM((count, EDGE, width), jnp.float32) for count in (3, 2, 2)
        ] + [VMEM((2, EDGE, width), jnp.int32), pltpu.SemaphoreType.DMA((11,))],
    )
    behind = from_behind(to_ahead, "tile", 1)
    shares = array(ports, 2 * depth // PLANES, rows, LANES)
    half = array(ports, depth // PLANES, rows, LANES)
    stage = [VMEM(half.shape, jnp.float32), pltpu.SemaphoreType.DMA((half.shape[1],))]
    packed, to_behind = call(
        functools.partial(early_kernel, ports),
        (electric, adjoint_electric, to_behind),
        (VMEM,) * 3,
        (shares, edge),
        (HBM, VMEM),
        cells,
        cells,
        stage,
    )
    ahead = from_behind(to_behind, "tile", -1)
    packed, drives = call(
        functools.partial(late_kernel, ports),
        (electric, magnetic, adjoint_electric, port_cells, push, packed),
        (VMEM,) * 3 + (SMEM, VMEM, HBM),
        (shares, half),
        (HBM, VMEM),
        60 * cells,
        cells * 4 * 11,
        stage,
        {5: 0},
    )
    (packed,) = call(
        functools.partial(rim_kernel, ports),
        (behind, ahead, *kept, drives, packed),
        (VMEM,) * 6 + (HBM,),
        (shares,),
        (HBM,),
        2 * cells,
        cells,
        stage,
        {6: 0},
    )
    gathered = lax.all_to_all(packed, "port", 0, 0, tiled=True)
    new_electric, new_magnetic, factors = call(
        functools.partial(field_kernel, ports),
        (adjoint_electric, adjoint_magnetic, region_labels, behind, ahead, permittivity_table, conductivity_table),
        (VMEM, HBM_BLOCK, HBM_BLOCK, VMEM, VMEM) + (SMEM,) * 2,
        (array(1, 3, depth, rows, width), array(1, 3, depth, rows, width), array(3, depth // PLANES, rows, LANES)),
        (HBM_BLOCK, HBM_BLOCK, VMEM),
        80 * cells,
        cells * 4 * 13,
    )
    gradient = array(depth, rows, share)
    gradient_perm, gradient_cond = call(
        gradient_kernel,
        (gathered, factors),
        (VMEM,) * 2,
        (gradient, gradient),
        (HBM_BLOCK,) * 2,
        4 * cells,
        cells * 4 * 3,
    )
    return (new_electric, new_magnetic, gradient_perm, gradient_cond)


def solution(mesh):
    return jax.shard_map(
        on_device,
        mesh=mesh,
        in_specs=(
            P("port", None, None, "tile", None),
            P("port", None, None, "tile", None),
            P("port", None, None, "tile", None),
            P("port", None, None, "tile", None),
            P(None, "tile", None),
            P(),
            P(),
            P("port"),
            P("port", None),
        ),
        out_specs=(
            P("port", None, None, "tile", None),
            P("port", None, None, "tile", None),
            P(None, "tile", "port"),
            P(None, "tile", "port"),
        ),
        check_vma=False,
    )
```

```python
import functools

import jax
import jax.numpy as jnp
from jax import lax
from jax.experimental import pallas as pl
from jax.experimental.pallas import tpu as pltpu
from jax.sharding import PartitionSpec as P

TIMESTEP = 0.5
HALF_STEP = 0.25
PLANES = 3
LANES = 128
EDGE = 8
VMEM_LIMIT = 12 << 20
VMEM = pltpu.VMEM
SMEM = pltpu.SMEM
HBM = pltpu.HBM
HBM_BLOCK = None


def from_behind(value, axis, steps):
    count = lax.axis_size(axis)
    first, last = (max(0, -steps), min(count, count - steps))
    return lax.ppermute(value, axis, [(source, source + steps) for source in range(first, last)])


def lane_iota(shape):
    return lax.broadcasted_iota(jnp.int32, shape, len(shape) - 1)


def row_iota(shape):
    return lax.broadcasted_iota(jnp.int32, shape, len(shape) - 2)


def lane_next(value):
    width = value.shape[1]
    return jnp.where(lane_iota(value.shape) == width - 1, 0.0, pltpu.roll(value, width - 1, 1))


def lane_prev(value):
    return jnp.where(lane_iota(value.shape) == 0, 0.0, pltpu.roll(value, 1, 1))


def row_next(value, beyond):
    rows = value.shape[0]
    return jnp.where(row_iota(value.shape) == rows - 1, beyond, pltpu.roll(value, rows - 1, 0))


def row_prev(value, before):
    return jnp.where(row_iota(value.shape) == 0, before, pltpu.roll(value, 1, 0))


def look_up(labels, entries):
    count = len(entries)
    level = list(entries)
    bit = 1
    while len(level) > 1:
        odd = (labels & bit) != 0
        level = [
            jnp.where(odd, level[i + 1], level[i]) if i + 1 < len(level) else level[i]
            for i in range(0, len(level), 2)
        ]
        bit *= 2
    assert count <= bit
    return level[0]


def region_values(perm_ref, cond_ref):
    shape = (1, LANES)
    perm = [jnp.full(shape, perm_ref[r], jnp.float32) for r in range(perm_ref.shape[0])]
    cond = [jnp.full(shape, cond_ref[r], jnp.float32) for r in range(cond_ref.shape[0])]
    return perm, cond


def widen(entries, width):
    return [jnp.concatenate([entry] * (width // LANES), axis=1) for entry in entries]


def gains(perm_ref, cond_ref, width):
    perm, cond = region_values(perm_ref, cond_ref)
    denominator = [p + HALF_STEP * c for p, c in zip(perm, cond, strict=True)]
    source = [TIMESTEP / d for d in denominator]
    update = [(p - HALF_STEP * c) / d for p, c, d in zip(perm, cond, denominator, strict=True)]
    return widen(source, width), widen(update, width)


def edge_kernel(e, m, ae, am, labels, perms, conds, amplitude, to_ahead, to_behind, ae_last, ae_first, e_first, push, perm, cond, force, e_last, m_last, am_last, marks, sems):
    _, _, depth, rows, width = e.shape
    last = rows - 1
    planes = pl.ds(0, depth)
    moves = (
        (perms, perm),
        (conds, cond),
        (labels.at[:, last], marks.at[0, planes]),
        (labels.at[:, 0], marks.at[1, planes]),
        (e.at[0, :, :, last], e_last.at[:, planes]),
        (m.at[0, pl.ds(1, 2), :, last], m_last.at[:, planes]),
        (ae.at[0, :, :, last], ae_last.at[:, planes]),
        (am.at[0, pl.ds(1, 2), :, last], am_last.at[:, planes]),
        (ae.at[0, pl.ds(1, 2), :, 0], ae_first.at[:, planes]),
        (e.at[0, pl.ds(1, 2), :, 0], e_first.at[:, planes]),
        (amplitude, force),
    )
    copies = [pltpu.make_async_copy(src, dst, sems.at[i]) for i, (src, dst) in enumerate(moves)]
    for copy in copies:
        copy.start()
    for ref in (e_last, ae_last):
        ref[0, depth:, :] = jnp.zeros((EDGE - depth, width), jnp.float32)

    def wait(first, count):
        for copy in copies[first : first + count]:
            copy.wait()

    def plane_next(value):
        return pltpu.roll(value, EDGE - 1, 0)

    wait(0, 2)
    source, _ = gains(perm, cond, width)
    wait(2, 2)
    last_gain, first_gain = (look_up(marks[i], source) for i in range(2))
    wait(4, 2)
    ex, ey, ez = (e_last[c] for c in range(3))
    up = [
        m_last[0] - TIMESTEP * ((plane_next(ex) - ex) + ez),
        m_last[1] + TIMESTEP * (ey + (lane_next(ex) - ex)),
    ]
    wait(6, 2)
    sx, sy, sz = (last_gain * ae_last[c] for c in range(3))
    up += [
        am_last[0] + ((plane_next(sx) - sx) + sz),
        am_last[1] - (sy + (lane_next(sx) - sx)),
    ]
    wait(8, 3)
    for c in range(3):
        push[c] = jnp.full(push.shape[1:], force[0, c], jnp.float32)
    down = (e_first[0], e_first[1], first_gain * ae_first[0], first_gain * ae_first[1])
    for i, (above, below) in enumerate(zip(up, down, strict=True)):
        at = i * depth
        to_ahead[at : at + depth, :] = above[:depth]
        to_behind[at : at + depth, :] = below[:depth]


def line_of(ref):
    return lambda i: ref[i : i + 1, :]


def pack(planes, share, ports):
    rows = planes[0].shape[0]
    lane = lane_iota((rows, LANES))
    blocks = []
    for port in range(ports):
        tile, offset = divmod(port * share, LANES)
        pieces = []
        for j, plane in enumerate(planes):
            piece = plane[:, tile * LANES : (tile + 1) * LANES]
            if offset + share > LANES:
                piece = jnp.where(
                    lane >= offset, piece, plane[:, (tile + 1) * LANES : (tile + 2) * LANES]
                )
            shift = (j * share - offset) % LANES
            pieces.append(pltpu.roll(piece, shift, 1) if shift else piece)
        block = pieces[-1]
        for j in range(len(planes) - 2, -1, -1):
            block = jnp.where(lane < (j + 1) * share, pieces[j], block)
        blocks.append(block)
    return blocks


def drive_shares(ports, e, m, ae, drives):
    _, _, depth, rows, width = e.shape
    share = width // ports
    def at(ref, c, z):
        return ref[0, c, z] if z < depth else jnp.zeros((rows, width), jnp.float32)

    zero = jnp.zeros((rows, width), jnp.float32)
    fx_prev, fy_prev = zero, zero
    sums = []
    for z in range(depth):
        ex, ey, ez = (at(e, c, z) for c in range(3))
        fx = at(m, 0, z) - TIMESTEP * ((lane_next(ez) - ez) - (at(e, 1, z + 1) - ey))
        fy = at(m, 1, z) - TIMESTEP * ((at(e, 0, z + 1) - ex) - (row_next(ez, 0.0) - ez))
        fz = at(m, 2, z) - TIMESTEP * ((row_next(ey, 0.0) - ey) - (lane_next(ex) - ex))
        drive_x = ((fz - lane_prev(fz)) - (fy - fy_prev))
        drive_y = ((fx - fx_prev) - (fz - row_prev(fz, 0.0)))
        drive_z = ((fy - row_prev(fy, 0.0)) - (fx - lane_prev(fx)))
        ax, ay, az = (at(ae, c, z) for c in range(3))
        sums.append(ax * drive_x + ay * drive_y + az * drive_z)
        fx_prev, fy_prev = fx, fy
        if z % PLANES == PLANES - 1:
            for port, block in enumerate(pack(sums, share, ports)):
                drives[port, z // PLANES] = block
            sums = []


def at_seam():
    return lax.axis_index("tile") == lax.axis_size("tile") // 2


def electric_shares(ports, e, ae, packed, stage, sems):
    _, _, depth, _, width = e.shape
    groups = depth // PLANES
    copies = []
    for group in range(groups):
        planes = []
        for z in range(group * PLANES, (group + 1) * PLANES):
            ax, ay, az = (ae[0, c, z] for c in range(3))
            planes.append(ax * e[0, 0, z] + ay * e[0, 1, z] + az * e[0, 2, z])
        for port, block in enumerate(pack(planes, width // ports, ports)):
            stage[port, group] = block
        copies.append(pltpu.make_async_copy(stage.at[:, group], packed.at[:, group], sems.at[group]))
        copies[-1].start()
    return copies


def all_shares(ports, e, m, ae, packed, drives, stage, sems):
    copies = electric_shares(ports, e, ae, packed, stage, sems)
    drive_shares(ports, e, m, ae, drives)
    for copy in copies:
        copy.wait()


def early_kernel(ports, e, m, ae, edge, packed, drives, edge_out, stage, sems):
    edge_out[...] = edge[...]

    @pl.when(at_seam())
    def _():
        all_shares(ports, e, m, ae, packed, drives, stage, sems)


def late_kernel(ports, e, m, ae, packed_in, drives_in, packed, drives, stage, sems):
    del packed_in

    @pl.when(at_seam())
    def _():
        drives[...] = drives_in[...]

    @pl.when(jnp.logical_not(at_seam()))
    def _():
        all_shares(ports, e, m, ae, packed, drives, stage, sems)


def subtract_source(share, ae, cells, amplitude, drives):
    _, _, depth, rows, width = ae.shape
    own = rows * width
    plane_cells = lax.axis_size("tile") * own
    z = lax.div(cells[0], plane_cells)
    local = cells[0] - z * plane_cells - lax.axis_index("tile") * own

    @pl.when(jnp.logical_and(local >= 0, local < own))
    def _():
        x = lax.div(local, width)
        y = local - x * width
        slot, group = lax.div(y, share), lax.div(z, PLANES)
        at = (z - group * PLANES) * share + (y - slot * share)
        line = jnp.zeros((1, width), jnp.float32)
        for c in range(3):
            push = jnp.concatenate([amplitude[c, :1]] * (width // LANES), axis=1)
            line = line + push * ae[0, c, z, pl.ds(x, 1), :]
        amount = jnp.sum(jnp.where(lane_iota((1, width)) == y, line, 0.0), axis=1, keepdims=True)
        change = jnp.where(lane_iota((1, LANES)) == at, amount, 0.0)
        drives[slot, group, pl.ds(x, 1), :] = drives[slot, group, pl.ds(x, 1), :] - change


def rim_kernel(ports, behind, ahead, ae_last, ae_first, e_first, ae, cells, amplitude, drives, packed, patched, stage, sems):
    del packed
    depth = behind.shape[0] // 4
    width = behind.shape[1]
    rows = patched.shape[2]
    groups = depth // PLANES
    share = width // ports
    inside = jnp.where(lax.axis_index("tile") > 0, 1.0, 0.0)

    def part(ref, i):
        return ref[i * depth : (i + 1) * depth, :]

    at_y, at_z = TIMESTEP * part(ahead, 1), -TIMESTEP * part(ahead, 0)
    plane_before = jnp.concatenate([jnp.zeros((1, width), jnp.float32), at_y[:-1]], axis=0)
    drive_x = (at_z - lane_prev(at_z)) - (at_y - plane_before)
    ax, ay, az = (ae_last[c, :depth] for c in range(3))
    last = ax * drive_x - ay * at_z + az * at_y
    prev_y = inside * (part(behind, 0) + TIMESTEP * e_first[1, :depth])
    prev_z = inside * (part(behind, 1) - TIMESTEP * e_first[0, :depth])
    first = ae_first[0, :depth] * prev_z - ae_first[1, :depth] * prev_y
    planes = [
        jnp.concatenate(
            [side[g * PLANES + j : g * PLANES + j + 1] for side in (first, last) for g in range(groups)], axis=0
        )
        for j in range(PLANES)
    ]
    row = row_iota((rows, LANES))
    inner = jnp.logical_and(row > 0, row < rows - 1)
    for port, block in enumerate(pack(planes, share, ports)):
        for g in range(groups):
            edges = jnp.where(row == 0, block[g : g + 1], block[groups + g : groups + g + 1])
            stage[port, g] = drives[port, g] + jnp.where(inner, 0.0, edges)
    subtract_source(share, ae, cells, amplitude, stage)
    copies = [
        pltpu.make_async_copy(stage.at[:, g], patched.at[:, groups + g], sems.at[g]) for g in range(groups)
    ]
    for copy in copies:
        copy.start()
    for copy in copies:
        copy.wait()


def share_factors(ports, labels, perm, cond, factors):
    depth, rows, width = labels.shape
    share = width // ports
    begin = lax.axis_index("port") * share
    perms, conds = region_values(perm, cond)
    denominators = [p + HALF_STEP * c for p, c in zip(perms, conds, strict=True)]
    scales = [TIMESTEP / (d * d) for d in denominators]
    lane = lane_iota((rows, LANES))
    for group in range(depth // PLANES):
        mine = None
        for j in range(PLANES - 1, -1, -1):
            shift = lax.rem(width - begin + j * share, width)
            piece = pltpu.roll(labels[group * PLANES + j], shift, 1)[:, :LANES]
            mine = piece if mine is None else jnp.where(lane < (j + 1) * share, piece, mine)
        for i, entries in enumerate((scales, perms, conds)):
            factors[i, group] = look_up(mine, entries)


def field_kernel(ports, ae, am, labels, behind, ahead, perm, cond, new_e, new_m, factors):
    depth, rows, width = labels.shape
    share_factors(ports, labels, perm, cond, factors)
    source, update = gains(perm, cond, width)
    above, below = line_of(behind), line_of(ahead)
    inside = jnp.where(lax.axis_index("tile") > 0, 1.0, 0.0)
    zero = jnp.zeros((rows, width), jnp.float32)

    def scaled(z):
        if z == depth:
            return [zero] * 3
        gain = look_up(labels[z], source)
        return [gain * ae[0, c, z] for c in range(3)]

    nx_prev, ny_prev = zero, zero
    here = scaled(0)
    for z in range(depth):
        after = scaled(z + 1)
        sx, sy, sz = here
        next_y = below(2 * depth + z)
        next_z = below(3 * depth + z)
        nx = am[0, 0, z] + ((lane_next(sz) - sz) - (after[1] - sy))
        ny = am[0, 1, z] + ((after[0] - sx) - (row_next(sz, next_z) - sz))
        nz = am[0, 2, z] + ((row_next(sy, next_y) - sy) - (lane_next(sx) - sx))
        prev_y = inside * (above(2 * depth + z) - sz[0:1])
        prev_z = inside * (above(3 * depth + z) + sy[0:1])
        new_m[0, 0, z] = nx
        new_m[0, 1, z] = ny
        new_m[0, 2, z] = nz
        gain = look_up(labels[z], update)
        new_e[0, 0, z] = gain * ae[0, 0, z] - TIMESTEP * ((nz - lane_prev(nz)) - (ny - ny_prev))
        new_e[0, 1, z] = gain * ae[0, 1, z] - TIMESTEP * ((nx - nx_prev) - (nz - row_prev(nz, prev_z)))
        new_e[0, 2, z] = gain * ae[0, 2, z] - TIMESTEP * ((ny - row_prev(ny, prev_y)) - (nx - lane_prev(nx)))
        nx_prev, ny_prev = nx, ny
        here = after


def gradient_kernel(gathered, factors, grad_perm, grad_cond):
    ports, slabs, rows, _ = gathered.shape
    depth, _, share = grad_perm.shape
    groups = depth // PLANES
    sums = []
    for slab in range(slabs):
        total = gathered[0, slab]
        for port in range(1, ports):
            total = total + gathered[port, slab]
        sums.append(total)
    for group in range(groups):
        corr_a, corr_b = sums[group], sums[groups + group]
        factor, permittivity, conductivity = (factors[i, group] for i in range(3))
        by_perm = factor * (conductivity * corr_a - corr_b)
        by_cond = factor * (-permittivity * corr_a - HALF_STEP * corr_b)
        for j in range(PLANES):
            for ref, value in ((grad_perm, by_perm), (grad_cond, by_cond)):
                moved = pltpu.roll(value, LANES - j * share, 1) if j else value
                ref[group * PLANES + j] = moved[:, :share]


def call(kernel, inputs, spaces, outs, out_spaces, flops, moved, scratch=(), aliases=()):
    inputs = [pltpu.with_memory_space_constraint(x, space) if space in (VMEM, HBM) else x for x, space in zip(inputs, spaces, strict=True)]
    return pl.pallas_call(
        kernel,
        out_shape=tuple(space(out.shape, out.dtype) if space in (VMEM, HBM) else out for out, space in zip(outs, out_spaces, strict=True)),
        in_specs=[pl.BlockSpec(memory_space=VMEM if space is HBM_BLOCK else space) for space in spaces],
        out_specs=tuple(pl.BlockSpec(memory_space=VMEM if space is HBM_BLOCK else space) for space in out_spaces),
        scratch_shapes=scratch,
        input_output_aliases=dict(aliases),
        compiler_params=pltpu.CompilerParams(vmem_limit_bytes=VMEM_LIMIT),
        cost_estimate=pl.CostEstimate(flops=flops, bytes_accessed=moved, transcendentals=0),
    )(*inputs)


def on_device(
    electric,
    magnetic,
    adjoint_electric,
    adjoint_magnetic,
    region_labels,
    permittivity_table,
    conductivity_table,
    port_cells,
    port_amplitude,
):
    depth, rows, width = region_labels.shape
    ports = lax.axis_size("port")
    share = width // ports
    cells = depth * rows * width

    def array(*shape):
        return jax.ShapeDtypeStruct(shape, jnp.float32)

    edge = array(4 * depth, width)
    to_ahead, to_behind, *kept, push = call(
        edge_kernel,
        (electric, magnetic, adjoint_electric, adjoint_magnetic, region_labels, permittivity_table, conductivity_table, port_amplitude),
        (HBM,) * 8,
        (edge, edge) + tuple(array(count, EDGE, width) for count in (3, 2, 2)) + (array(3, EDGE, LANES),),
        (VMEM,) * 6,
        10 * cells,
        cells * 4 * 14,
        [SMEM(permittivity_table.shape, jnp.float32)] * 2 + [SMEM(port_amplitude.shape, jnp.float32)] + [
            VMEM((count, EDGE, width), jnp.float32) for count in (3, 2, 2)
        ] + [VMEM((2, EDGE, width), jnp.int32), pltpu.SemaphoreType.DMA((11,))],
    )
    behind = from_behind(to_ahead, "tile", 1)
    shares = array(ports, 2 * depth // PLANES, rows, LANES)
    half = array(ports, depth // PLANES, rows, LANES)
    stage = [VMEM(half.shape, jnp.float32), pltpu.SemaphoreType.DMA((half.shape[1],))]
    fields = (electric, magnetic, adjoint_electric)
    packed, drives, to_behind = call(
        functools.partial(early_kernel, ports),
        (*fields, to_behind),
        (VMEM,) * 4,
        (shares, half, edge),
        (HBM, VMEM, VMEM),
        cells,
        cells,
        stage,
    )
    ahead = from_behind(to_behind, "tile", -1)
    packed, drives = call(
        functools.partial(late_kernel, ports),
        (*fields, packed, drives),
        (VMEM,) * 3 + (HBM, VMEM),
        (shares, half),
        (HBM, VMEM),
        60 * cells,
        cells * 4 * 11,
        stage,
        {3: 0},
    )
    (packed,) = call(
        functools.partial(rim_kernel, ports),
        (behind, ahead, *kept, adjoint_electric, port_cells, push, drives, packed),
        (VMEM,) * 6 + (SMEM, VMEM, VMEM, HBM),
        (shares,),
        (HBM,),
        2 * cells,
        cells,
        stage,
        {9: 0},
    )
    gathered = lax.all_to_all(packed, "port", 0, 0, tiled=True)
    new_electric, new_magnetic, factors = call(
        functools.partial(field_kernel, ports),
        (adjoint_electric, adjoint_magnetic, region_labels, behind, ahead, permittivity_table, conductivity_table),
        (VMEM, HBM_BLOCK, HBM_BLOCK, VMEM, VMEM) + (SMEM,) * 2,
        (array(1, 3, depth, rows, width), array(1, 3, depth, rows, width), array(3, depth // PLANES, rows, LANES)),
        (HBM_BLOCK, HBM_BLOCK, VMEM),
        80 * cells,
        cells * 4 * 13,
    )
    gradient = array(depth, rows, share)
    gradient_perm, gradient_cond = call(
        gradient_kernel,
        (gathered, factors),
        (VMEM,) * 2,
        (gradient, gradient),
        (HBM_BLOCK,) * 2,
        4 * cells,
        cells * 4 * 3,
    )
    return (new_electric, new_magnetic, gradient_perm, gradient_cond)


def solution(mesh):
    return jax.shard_map(
        on_device,
        mesh=mesh,
        in_specs=(
            P("port", None, None, "tile", None),
            P("port", None, None, "tile", None),
            P("port", None, None, "tile", None),
            P("port", None, None, "tile", None),
            P(None, "tile", None),
            P(),
            P(),
            P("port"),
            P("port", None),
        ),
        out_specs=(
            P("port", None, None, "tile", None),
            P("port", None, None, "tile", None),
            P(None, "tile", "port"),
            P(None, "tile", "port"),
        ),
        check_vma=False,
    )
```

```python
import functools

import jax
import jax.numpy as jnp
from jax import lax
from jax.experimental import pallas as pl
from jax.experimental.pallas import tpu as pltpu
from jax.sharding import PartitionSpec as P

TIMESTEP = 0.5
HALF_STEP = 0.25
PLANES = 3
LANES = 128
EDGE = 8
VMEM_LIMIT = 12 << 20
VMEM = pltpu.VMEM
SMEM = pltpu.SMEM
HBM = pltpu.HBM
HBM_BLOCK = None


def from_behind(value, axis, steps):
    count = lax.axis_size(axis)
    first, last = (max(0, -steps), min(count, count - steps))
    return lax.ppermute(value, axis, [(source, source + steps) for source in range(first, last)])


def lane_iota(shape):
    return lax.broadcasted_iota(jnp.int32, shape, len(shape) - 1)


def row_iota(shape):
    return lax.broadcasted_iota(jnp.int32, shape, len(shape) - 2)


def lane_next(value):
    width = value.shape[1]
    return jnp.where(lane_iota(value.shape) == width - 1, 0.0, pltpu.roll(value, width - 1, 1))


def lane_prev(value):
    return jnp.where(lane_iota(value.shape) == 0, 0.0, pltpu.roll(value, 1, 1))


def row_next(value, beyond):
    rows = value.shape[0]
    return jnp.where(row_iota(value.shape) == rows - 1, beyond, pltpu.roll(value, rows - 1, 0))


def row_prev(value, before):
    return jnp.where(row_iota(value.shape) == 0, before, pltpu.roll(value, 1, 0))


def look_up(labels, entries):
    count = len(entries)
    level = list(entries)
    bit = 1
    while len(level) > 1:
        odd = (labels & bit) != 0
        level = [
            jnp.where(odd, level[i + 1], level[i]) if i + 1 < len(level) else level[i]
            for i in range(0, len(level), 2)
        ]
        bit *= 2
    assert count <= bit
    return level[0]


def region_values(perm_ref, cond_ref):
    shape = (1, LANES)
    perm = [jnp.full(shape, perm_ref[r], jnp.float32) for r in range(perm_ref.shape[0])]
    cond = [jnp.full(shape, cond_ref[r], jnp.float32) for r in range(cond_ref.shape[0])]
    return perm, cond


def widen(entries, width):
    return [jnp.concatenate([entry] * (width // LANES), axis=1) for entry in entries]


def gains(perm_ref, cond_ref, width):
    perm, cond = region_values(perm_ref, cond_ref)
    denominator = [p + HALF_STEP * c for p, c in zip(perm, cond, strict=True)]
    source = [TIMESTEP / d for d in denominator]
    update = [(p - HALF_STEP * c) / d for p, c, d in zip(perm, cond, denominator, strict=True)]
    return widen(source, width), widen(update, width)


def edge_kernel(e, m, ae, am, labels, perms, conds, amplitude, to_ahead, to_behind, ae_last, ae_first, e_first, push, perm, cond, force, e_last, m_last, am_last, marks, sems):
    _, _, depth, rows, width = e.shape
    last = rows - 1
    planes = pl.ds(0, depth)
    for ref in (ae_last, ae_first, e_first, e_last, m_last, am_last):
        ref[:, depth:, :] = jnp.zeros((ref.shape[0], EDGE - depth, width), jnp.float32)
    moves = (
        (perms, perm),
        (conds, cond),
        (amplitude, force),
        (ae.at[0, :, :, last], ae_last.at[:, planes]),
        (ae.at[0, pl.ds(1, 2), :, 0], ae_first.at[:, planes]),
        (labels.at[:, last], marks.at[0, planes]),
        (labels.at[:, 0], marks.at[1, planes]),
        (e.at[0, :, :, last], e_last.at[:, planes]),
        (e.at[0, pl.ds(1, 2), :, 0], e_first.at[:, planes]),
        (m.at[0, pl.ds(1, 2), :, last], m_last.at[:, planes]),
        (am.at[0, pl.ds(1, 2), :, last], am_last.at[:, planes]),
    )
    copies = [pltpu.make_async_copy(src, dst, sems.at[i]) for i, (src, dst) in enumerate(moves)]
    for copy in copies:
        copy.start()
    def plane_next(value):
        return pltpu.roll(value, EDGE - 1, 0)

    for copy in copies:
        copy.wait()
    source, _ = gains(perm, cond, width)
    for c in range(3):
        push[c] = jnp.full(push.shape[1:], force[0, c], jnp.float32)
    last_gain, first_gain = (look_up(marks[i], source) for i in range(2))
    ex, ey, ez = (e_last[c] for c in range(3))
    sx, sy, sz = (last_gain * ae_last[c] for c in range(3))
    up = (
        m_last[0] - TIMESTEP * ((plane_next(ex) - ex) + ez),
        m_last[1] + TIMESTEP * (ey + (lane_next(ex) - ex)),
        am_last[0] + ((plane_next(sx) - sx) + sz),
        am_last[1] - (sy + (lane_next(sx) - sx)),
    )
    down = (e_first[0], e_first[1], first_gain * ae_first[0], first_gain * ae_first[1])
    for i, (above, below) in enumerate(zip(up, down, strict=True)):
        at = i * depth
        to_ahead[at : at + depth, :] = above[:depth]
        to_behind[at : at + depth, :] = below[:depth]


def line_of(ref):
    return lambda i: ref[i : i + 1, :]


def pack(planes, share, ports):
    rows = planes[0].shape[0]
    lane = lane_iota((rows, LANES))
    blocks = []
    for port in range(ports):
        tile, offset = divmod(port * share, LANES)
        pieces = []
        for j, plane in enumerate(planes):
            piece = plane[:, tile * LANES : (tile + 1) * LANES]
            if offset + share > LANES:
                piece = jnp.where(
                    lane >= offset, piece, plane[:, (tile + 1) * LANES : (tile + 2) * LANES]
                )
            shift = (j * share - offset) % LANES
            pieces.append(pltpu.roll(piece, shift, 1) if shift else piece)
        block = pieces[-1]
        for j in range(len(planes) - 2, -1, -1):
            block = jnp.where(lane < (j + 1) * share, pieces[j], block)
        blocks.append(block)
    return blocks


def drive_shares(ports, e, m, ae, cells, amplitude, drives):
    _, _, depth, rows, width = e.shape
    share = width // ports
    tile = lax.axis_index("tile")
    plane_cells = lax.axis_size("tile") * rows * width
    target = cells[0] - tile * (rows * width)
    push = [jnp.concatenate([amplitude[c, :1]] * (width // LANES), axis=1) for c in range(3)]
    position = row_iota((rows, width)) * width + lane_iota((rows, width))

    def at(ref, c, z):
        return ref[0, c, z] if z < depth else jnp.zeros((rows, width), jnp.float32)

    zero = jnp.zeros((rows, width), jnp.float32)
    fx_prev, fy_prev = zero, zero
    sums = []
    for z in range(depth):
        ex, ey, ez = (at(e, c, z) for c in range(3))
        fx = at(m, 0, z) - TIMESTEP * ((lane_next(ez) - ez) - (at(e, 1, z + 1) - ey))
        fy = at(m, 1, z) - TIMESTEP * ((at(e, 0, z + 1) - ex) - (row_next(ez, 0.0) - ez))
        fz = at(m, 2, z) - TIMESTEP * ((row_next(ey, 0.0) - ey) - (lane_next(ex) - ex))
        hit = position == target - z * plane_cells
        drive_x = ((fz - lane_prev(fz)) - (fy - fy_prev)) - jnp.where(hit, push[0], 0.0)
        drive_y = ((fx - fx_prev) - (fz - row_prev(fz, 0.0))) - jnp.where(hit, push[1], 0.0)
        drive_z = ((fy - row_prev(fy, 0.0)) - (fx - lane_prev(fx))) - jnp.where(
            hit, push[2], 0.0
        )
        ax, ay, az = (at(ae, c, z) for c in range(3))
        sums.append(ax * drive_x + ay * drive_y + az * drive_z)
        fx_prev, fy_prev = fx, fy
        if z % PLANES == PLANES - 1:
            for port, block in enumerate(pack(sums, share, ports)):
                drives[port, z // PLANES] = block
            sums = []


def at_seam():
    return lax.axis_index("tile") == lax.axis_size("tile") // 2


def electric_shares(ports, e, ae, packed, stage, sems):
    _, _, depth, _, width = e.shape
    groups = depth // PLANES
    copies = []
    for group in range(groups):
        planes = []
        for z in range(group * PLANES, (group + 1) * PLANES):
            ax, ay, az = (ae[0, c, z] for c in range(3))
            planes.append(ax * e[0, 0, z] + ay * e[0, 1, z] + az * e[0, 2, z])
        for port, block in enumerate(pack(planes, width // ports, ports)):
            stage[port, group] = block
        copies.append(pltpu.make_async_copy(stage.at[:, group], packed.at[:, group], sems.at[group]))
        copies[-1].start()
    return copies


def early_kernel(ports, e, ae, edge, packed, edge_out, stage, sems):
    edge_out[...] = edge[...]

    @pl.when(at_seam())
    def _():
        for copy in electric_shares(ports, e, ae, packed, stage, sems):
            copy.wait()


def late_kernel(ports, e, m, ae, cells, amplitude, packed_in, packed, drives, stage, sems):
    del packed_in

    @pl.when(jnp.logical_not(at_seam()))
    def _():
        copies = electric_shares(ports, e, ae, packed, stage, sems)
        drive_shares(ports, e, m, ae, cells, amplitude, drives)
        for copy in copies:
            copy.wait()

    @pl.when(at_seam())
    def _():
        drive_shares(ports, e, m, ae, cells, amplitude, drives)


def rim_kernel(ports, behind, ahead, ae_last, ae_first, e_first, drives, packed, patched, stage, sems):
    del packed
    depth = behind.shape[0] // 4
    width = behind.shape[1]
    rows = patched.shape[2]
    groups = depth // PLANES
    share = width // ports
    inside = jnp.where(lax.axis_index("tile") > 0, 1.0, 0.0)

    def part(ref, i):
        return ref[i * depth : (i + 1) * depth, :]

    at_y, at_z = TIMESTEP * part(ahead, 1), -TIMESTEP * part(ahead, 0)
    plane_before = jnp.concatenate([jnp.zeros((1, width), jnp.float32), at_y[:-1]], axis=0)
    drive_x = (at_z - lane_prev(at_z)) - (at_y - plane_before)
    ax, ay, az = (ae_last[c, :depth] for c in range(3))
    last = ax * drive_x - ay * at_z + az * at_y
    prev_y = inside * (part(behind, 0) + TIMESTEP * e_first[1, :depth])
    prev_z = inside * (part(behind, 1) - TIMESTEP * e_first[0, :depth])
    first = ae_first[0, :depth] * prev_z - ae_first[1, :depth] * prev_y
    planes = [
        jnp.concatenate(
            [side[g * PLANES + j : g * PLANES + j + 1] for side in (first, last) for g in range(groups)], axis=0
        )
        for j in range(PLANES)
    ]
    blocks = pack(planes, share, ports)
    row = row_iota((rows, LANES))
    copies = []
    for g in range(groups):
        for port, block in enumerate(blocks):
            edges = jnp.where(row == 0, block[g : g + 1], block[groups + g : groups + g + 1])
            inner = jnp.logical_and(row > 0, row < rows - 1)
            stage[port, g] = drives[port, g] + jnp.where(inner, 0.0, edges)
        copies.append(pltpu.make_async_copy(stage.at[:, g], patched.at[:, groups + g], sems.at[g]))
        copies[-1].start()
    for copy in copies:
        copy.wait()


def share_factors(ports, labels, perm, cond, factors):
    depth, rows, width = labels.shape
    share = width // ports
    begin = lax.axis_index("port") * share
    perms, conds = region_values(perm, cond)
    denominators = [p + HALF_STEP * c for p, c in zip(perms, conds, strict=True)]
    scales = [TIMESTEP / (d * d) for d in denominators]
    lane = lane_iota((rows, LANES))
    for group in range(depth // PLANES):
        mine = None
        for j in range(PLANES - 1, -1, -1):
            shift = lax.rem(width - begin + j * share, width)
            piece = pltpu.roll(labels[group * PLANES + j], shift, 1)[:, :LANES]
            mine = piece if mine is None else jnp.where(lane < (j + 1) * share, piece, mine)
        for i, entries in enumerate((scales, perms, conds)):
            factors[i, group] = look_up(mine, entries)


def field_kernel(ports, ae, am, labels, behind, ahead, perm, cond, new_e, new_m, factors):
    depth, rows, width = labels.shape
    share_factors(ports, labels, perm, cond, factors)
    source, update = gains(perm, cond, width)
    above, below = line_of(behind), line_of(ahead)
    inside = jnp.where(lax.axis_index("tile") > 0, 1.0, 0.0)
    zero = jnp.zeros((rows, width), jnp.float32)

    def scaled(z):
        if z == depth:
            return [zero] * 3
        gain = look_up(labels[z], source)
        return [gain * ae[0, c, z] for c in range(3)]

    nx_prev, ny_prev = zero, zero
    here = scaled(0)
    for z in range(depth):
        after = scaled(z + 1)
        sx, sy, sz = here
        next_y = below(2 * depth + z)
        next_z = below(3 * depth + z)
        nx = am[0, 0, z] + ((lane_next(sz) - sz) - (after[1] - sy))
        ny = am[0, 1, z] + ((after[0] - sx) - (row_next(sz, next_z) - sz))
        nz = am[0, 2, z] + ((row_next(sy, next_y) - sy) - (lane_next(sx) - sx))
        prev_y = inside * (above(2 * depth + z) - sz[0:1])
        prev_z = inside * (above(3 * depth + z) + sy[0:1])
        new_m[0, 0, z] = nx
        new_m[0, 1, z] = ny
        new_m[0, 2, z] = nz
        gain = look_up(labels[z], update)
        new_e[0, 0, z] = gain * ae[0, 0, z] - TIMESTEP * ((nz - lane_prev(nz)) - (ny - ny_prev))
        new_e[0, 1, z] = gain * ae[0, 1, z] - TIMESTEP * ((nx - nx_prev) - (nz - row_prev(nz, prev_z)))
        new_e[0, 2, z] = gain * ae[0, 2, z] - TIMESTEP * ((ny - row_prev(ny, prev_y)) - (nx - lane_prev(nx)))
        nx_prev, ny_prev = nx, ny
        here = after


def gradient_kernel(gathered, factors, grad_perm, grad_cond, perm_stage, cond_stage, sems):
    ports = gathered.shape[0]
    depth, _, share = grad_perm.shape
    groups = depth // PLANES

    def total_of(slab):
        total = gathered[0, slab]
        for port in range(1, ports):
            total = total + gathered[port, slab]
        return total

    copies = []
    for group in range(groups):
        corr_a, corr_b = total_of(group), total_of(groups + group)
        factor, permittivity, conductivity = (factors[i, group] for i in range(3))
        by_perm = factor * (conductivity * corr_a - corr_b)
        by_cond = factor * (-permittivity * corr_a - HALF_STEP * corr_b)
        for j in range(PLANES):
            for ref, value in ((perm_stage, by_perm), (cond_stage, by_cond)):
                moved = pltpu.roll(value, LANES - j * share, 1) if j else value
                ref[group * PLANES + j] = moved[:, :share]
        part = pl.ds(group * PLANES, PLANES)
        for i, (src, dst) in enumerate(((perm_stage, grad_perm), (cond_stage, grad_cond))):
            copies.append(pltpu.make_async_copy(src.at[part], dst.at[part], sems.at[2 * group + i]))
            copies[-1].start()
    for copy in copies:
        copy.wait()


def call(kernel, inputs, spaces, outs, out_spaces, flops, moved, scratch=(), aliases=()):
    inputs = [pltpu.with_memory_space_constraint(x, space) if space in (VMEM, HBM) else x for x, space in zip(inputs, spaces, strict=True)]
    return pl.pallas_call(
        kernel,
        out_shape=tuple(space(out.shape, out.dtype) if space in (VMEM, HBM) else out for out, space in zip(outs, out_spaces, strict=True)),
        in_specs=[pl.BlockSpec(memory_space=VMEM if space is HBM_BLOCK else space) for space in spaces],
        out_specs=tuple(pl.BlockSpec(memory_space=VMEM if space is HBM_BLOCK else space) for space in out_spaces),
        scratch_shapes=scratch,
        input_output_aliases=dict(aliases),
        compiler_params=pltpu.CompilerParams(vmem_limit_bytes=VMEM_LIMIT),
        cost_estimate=pl.CostEstimate(flops=flops, bytes_accessed=moved, transcendentals=0),
    )(*inputs)


def on_device(
    electric,
    magnetic,
    adjoint_electric,
    adjoint_magnetic,
    region_labels,
    permittivity_table,
    conductivity_table,
    port_cells,
    port_amplitude,
):
    depth, rows, width = region_labels.shape
    ports = lax.axis_size("port")
    share = width // ports
    cells = depth * rows * width

    def array(*shape):
        return jax.ShapeDtypeStruct(shape, jnp.float32)

    edge = array(4 * depth, width)
    to_ahead, to_behind, *kept, push = call(
        edge_kernel,
        (electric, magnetic, adjoint_electric, adjoint_magnetic, region_labels, permittivity_table, conductivity_table, port_amplitude),
        (HBM,) * 8,
        (edge, edge) + tuple(array(count, EDGE, width) for count in (3, 2, 2)) + (array(3, EDGE, LANES),),
        (VMEM,) * 6,
        10 * cells,
        cells * 4 * 14,
        [SMEM(permittivity_table.shape, jnp.float32)] * 2 + [SMEM(port_amplitude.shape, jnp.float32)] + [
            VMEM((count, EDGE, width), jnp.float32) for count in (3, 2, 2)
        ] + [VMEM((2, EDGE, width), jnp.int32), pltpu.SemaphoreType.DMA((11,))],
    )
    behind = from_behind(to_ahead, "tile", 1)
    shares = array(ports, 2 * depth // PLANES, rows, LANES)
    half = array(ports, depth // PLANES, rows, LANES)
    stage = [VMEM(half.shape, jnp.float32), pltpu.SemaphoreType.DMA((half.shape[1],))]
    packed, to_behind = call(
        functools.partial(early_kernel, ports),
        (electric, adjoint_electric, to_behind),
        (VMEM,) * 3,
        (shares, edge),
        (HBM, VMEM),
        cells,
        cells,
        stage,
    )
    ahead = from_behind(to_behind, "tile", -1)
    packed, drives = call(
        functools.partial(late_kernel, ports),
        (electric, magnetic, adjoint_electric, port_cells, push, packed),
        (VMEM,) * 3 + (SMEM, VMEM, HBM),
        (shares, half),
        (HBM, VMEM),
        60 * cells,
        cells * 4 * 11,
        stage,
        {5: 0},
    )
    (packed,) = call(
        functools.partial(rim_kernel, ports),
        (behind, ahead, *kept, drives, packed),
        (VMEM,) * 6 + (HBM,),
        (shares,),
        (HBM,),
        2 * cells,
        cells,
        stage,
        {6: 0},
    )
    gathered = lax.all_to_all(packed, "port", 0, 0, tiled=True)
    new_electric, new_magnetic, factors = call(
        functools.partial(field_kernel, ports),
        (adjoint_electric, adjoint_magnetic, region_labels, behind, ahead, permittivity_table, conductivity_table),
        (VMEM, HBM_BLOCK, HBM_BLOCK, VMEM, VMEM) + (SMEM,) * 2,
        (array(1, 3, depth, rows, width), array(1, 3, depth, rows, width), array(3, depth // PLANES, rows, LANES)),
        (HBM_BLOCK, HBM_BLOCK, VMEM),
        80 * cells,
        cells * 4 * 13,
    )
    gradient = array(depth, rows, share)
    gradient_perm, gradient_cond = call(
        gradient_kernel,
        (gathered, factors),
        (VMEM,) * 2,
        (gradient, gradient),
        (HBM,) * 2,
        4 * cells,
        cells * 4 * 3,
        [VMEM(gradient.shape, jnp.float32)] * 2 + [pltpu.SemaphoreType.DMA((2 * depth // PLANES,))],
    )
    return (new_electric, new_magnetic, gradient_perm, gradient_cond)


def solution(mesh):
    return jax.shard_map(
        on_device,
        mesh=mesh,
        in_specs=(
            P("port", None, None, "tile", None),
            P("port", None, None, "tile", None),
            P("port", None, None, "tile", None),
            P("port", None, None, "tile", None),
            P(None, "tile", None),
            P(),
            P(),
            P("port"),
            P("port", None),
        ),
        out_specs=(
            P("port", None, None, "tile", None),
            P("port", None, None, "tile", None),
            P(None, "tile", "port"),
            P(None, "tile", "port"),
        ),
        check_vma=False,
    )
```
